32 devices in a mesh: dp: 8 (over z, core), seq: 4 (over y, x).
Axes of the slice: x: 2, y: 2, z: 4, core: 2. Of those that a mesh axis runs over, the one named last changes fastest.
Arguments:
- waveform: bfloat16 [32, 2560], P('dp', 'seq'), may hold values from -6 to 6
- lengths: int32 [8, 4], P('dp'), may hold values from 1 to 2560, 6400 in all within a row
- conv_one: bfloat16 [10, 512], replicated, may hold values from -2 to 2
- conv_two: bfloat16 [1536, 512], replicated, may hold values from -0.15625 to 0.15625
- gain_one: float32 [512], replicated, may hold values from 0.1 to 1.9
- shift_one: float32 [512], replicated, may hold values from -3 to 3
- gain_two: float32 [512], replicated, may hold values from 0.1 to 1.9
- shift_two: float32 [512], replicated, may hold values from -3 to 3
- cotangent: bfloat16 [32, 256, 512], P('dp', 'seq'), may hold values from -0.0625 to 0.0625
Outputs:
- features: bfloat16 [32, 256, 512], P('dp', 'seq')
- conv_one_grad: float32 [10, 512], replicated
- conv_two_grad: float32 [1536, 512], P('seq')
- norm_grads: float32 [4, 512], replicated
The draws below stay inside these ranges and needn't reach their ends.
Inputs may be any that keep to these rules, and one draw needn't show every extreme that they name: In each row of lengths the 4 lengths sum to 6400 and the longest is exactly 2560.
All inputs are finite; a program needn't handle non-finite values.
Results may differ from the reference program's by a relative error of at most 0.0054.
Values may be sent and summed in bfloat16 or wider, within the bound.
A program may use at most 64 MiB of HBM per device.

```python
import math
import jax
import jax.numpy as jnp
import numpy as np
from jax import lax

CH = 512
CLIPS = 4
MAXLEN = 2560
F2 = 256
ALLCLIPS = 32
TOTLEN = 6400
N_DP = 8


def block_scale(rng, shape, split, low, high):
    level, own = 1.0, jax.random.fold_in(rng, 6)
    for dim, blocks in split:
        draws = jnp.exp(jax.random.uniform(jax.random.fold_in(own, dim), (blocks,), jnp.float32, low / len(split), high / len(split)))
        level = level * jnp.repeat(draws, shape[dim] // blocks).reshape([-1 if axis == dim else 1 for axis in range(len(shape))])
    return level


def length_profile(amount, total, limit, lean):
    loads = [(1 << 20) // math.isqrt(rank ** lean) + 1 for rank in range(2, amount + 1)]
    rest, given = total - limit - (amount - 1), [1] * (amount - 1)
    while rest > 0:
        movable = [i for i in range(amount - 1) if given[i] < limit]
        pool, budget = sum([loads[i] for i in movable]), rest
        for i in movable:
            more = min(limit - given[i], max(1, budget * loads[i] // pool), rest)
            given[i] = given[i] + more
            rest = rest - more
    return np.array([limit] + given)


def uneven_parts(rng, count, total, reach, lean):
    if count == 2:
        one = jax.random.randint(rng, (), max(1, total - reach), min(reach, total - 1) + 1)
        return jnp.stack([one, total - one])
    tallies = jnp.asarray(length_profile(count, total, reach, lean), jnp.int32)
    pairs = (count - 1) // 2
    source_of, receiver = tallies[1:1 + 2 * pairs:2], tallies[2:2 + 2 * pairs:2]
    room = jnp.minimum(source_of - 1, reach - receiver)
    moved = jax.random.randint(jax.random.fold_in(rng, 1), (pairs,), 0, 1 << 20) % (room + 1)
    tallies = tallies.at[1:1 + 2 * pairs:2].set(source_of - moved).at[2:2 + 2 * pairs:2].set(receiver + moved)
    return tallies[jax.random.permutation(jax.random.fold_in(rng, 2), count)]


def gaussian(own_key, dims, deviation, reach, shards=(), held_as=jnp.bfloat16):
    entries = jax.random.normal(own_key, dims, jnp.float32) * deviation
    if len(shards) > 0:
        entries = block_scale(own_key, dims, shards, -0.22, 0.18) * entries
    return jnp.clip(entries, min=-reach, max=reach).astype(held_as)


def setup_inputs(seed: int = 0) -> dict:
    streams_of = jax.random.split(jax.random.key(seed), 10)
    waveform = gaussian(streams_of[0], (ALLCLIPS, MAXLEN), 1.0, 6.0, ((0, 8), (1, 4)))
    lengths = jax.vmap(lambda own: uneven_parts(own, CLIPS, TOTLEN, MAXLEN, 2))(jax.random.split(streams_of[1], N_DP)).reshape((N_DP, CLIPS)).astype(jnp.int32)
    conv_one = gaussian(streams_of[2], (10, CH), 10 ** -0.5, 2.0)
    conv_two = gaussian(streams_of[3], (3 * CH, CH), (3 * CH) ** -0.5, 0.15625)
    gain_one = jnp.clip(1.0 + 0.18 * jax.random.normal(streams_of[4], (CH,), jnp.float32), 0.1, 1.9)
    shift_one = gaussian(streams_of[5], (CH,), 0.5, 3.0, (), jnp.float32)
    gain_two = jnp.clip(1.0 + 0.18 * jax.random.normal(streams_of[6], (CH,), jnp.float32), 0.1, 1.9)
    shift_two = gaussian(streams_of[7], (CH,), 0.5, 3.0, (), jnp.float32)
    cotangent = gaussian(streams_of[8], (ALLCLIPS, F2, CH), (ALLCLIPS * F2) ** -0.5, 0.0625, ((0, 8), (1, 4)))
    return dict(waveform=waveform, lengths=lengths, conv_one=conv_one, conv_two=conv_two, gain_one=gain_one, shift_one=shift_one, gain_two=gain_two, shift_two=shift_two, cotangent=cotangent)


epsilon = 1e-05
root_half = 0.7071067811865476
normal_peak = 0.3989422804014327

def norm_forward(preact, gain_vector, offset):
    centre = preact - lax.optimization_barrier(jnp.mean(preact, axis=-1, keepdims=True))
    inverse = lax.rsqrt(lax.optimization_barrier(jnp.mean(centre * centre, axis=-1, keepdims=True)) + epsilon)
    normed = centre * inverse
    return (normed, inverse, normed * gain_vector + offset)

def gelu_slope(values):
    return 0.5 * (1.0 + lax.erf(values * root_half)) + values * jnp.exp(-0.5 * values * values) * normal_peak

def norm_backward(upstream, normed, inverse, gain_vector):
    scaled = upstream * gain_vector
    return inverse * (scaled - lax.optimization_barrier(jnp.mean(scaled, axis=-1, keepdims=True)) - normed * lax.optimization_barrier(jnp.mean(scaled * normed, axis=-1, keepdims=True)))

def clip_pass(wave_clip, length, conv_one, conv_two, gain_one, shift_one, gain_two, shift_two, cot_clip):
    total_frames = wave_clip.shape[0] // 5
    half_frames = total_frames // 2
    channels = conv_two.shape[1]
    padded = jnp.concatenate([wave_clip, jnp.zeros((5,), wave_clip.dtype)])
    blocks = padded.reshape(total_frames + 1, 5)
    patch_one = jnp.concatenate([blocks[:-1], blocks[1:]], axis=1)
    pre_one = jnp.dot(patch_one, conv_one, preferred_element_type=jnp.float32)
    normed_one, inverse_one, output_one = norm_forward(pre_one, gain_one, shift_one)
    active_one = jax.nn.gelu(output_one, approximate=False).astype(jnp.bfloat16)
    widened = jnp.concatenate([active_one, jnp.zeros((1, channels), active_one.dtype)], axis=0)
    patch_two = jnp.concatenate([active_one.reshape(half_frames, 2 * channels), widened[2::2]], axis=1)
    pre_two = jnp.dot(patch_two, conv_two, preferred_element_type=jnp.float32)
    normed_two, inverse_two, output_two = norm_forward(pre_two, gain_two, shift_two)
    first_frames = (length - 5) // 5
    second_frames = (first_frames - 1) // 2
    validity = (jnp.arange(half_frames, dtype=jnp.int32) < second_frames).astype(output_two.dtype)[:, None]
    features = (jax.nn.gelu(output_two, approximate=False) * validity).astype(jnp.bfloat16)
    upstream_two = cot_clip.astype(output_two.dtype) * validity * gelu_slope(output_two)
    dpre_two = norm_backward(upstream_two, normed_two, inverse_two, gain_two).astype(jnp.bfloat16)
    grad_two = jnp.dot(patch_two.T, dpre_two, preferred_element_type=jnp.float32)
    dpatch_two = jnp.dot(dpre_two, conv_two.T, preferred_element_type=jnp.float32)
    paired = dpatch_two[:, :2 * channels].reshape(half_frames, 2, channels)
    onward = dpatch_two[:, 2 * channels:]
    carried = jnp.concatenate([jnp.zeros((1, channels), onward.dtype), onward[:-1]], axis=0)
    dact_one = jnp.stack([paired[:, 0] + carried, paired[:, 1]], axis=1).reshape(total_frames, channels)
    upstream_one = dact_one * gelu_slope(output_one)
    dpre_one = norm_backward(upstream_one, normed_one, inverse_one, gain_one)
    grad_one = jnp.dot(patch_one.astype(dpre_one.dtype).T, dpre_one, precision=lax.Precision.HIGHEST)
    norm_terms = jnp.stack([lax.optimization_barrier(jnp.sum(upstream_one * normed_one, 0)), lax.optimization_barrier(jnp.sum(upstream_one, 0)), lax.optimization_barrier(jnp.sum(upstream_two * normed_two, 0)), lax.optimization_barrier(jnp.sum(upstream_two, 0))])
    return (features, grad_one, grad_two, norm_terms)

def reference(waveform, lengths, conv_one, conv_two, gain_one, shift_one, gain_two, shift_two, cotangent):
    flat_lengths = lengths.reshape(-1)
    channels = conv_two.shape[1]

    def per_clip(totals, inputs):
        wave_clip, length, cot_clip = inputs
        features, grad_one, grad_two, norm_terms = clip_pass(wave_clip, length, conv_one, conv_two, gain_one, shift_one, gain_two, shift_two, cot_clip)
        return ((totals[0] + grad_one, totals[1] + grad_two, totals[2] + norm_terms), features)
    initial = (jnp.zeros((10, channels), jnp.float32), jnp.zeros((3 * channels, channels), jnp.float32), jnp.zeros((4, channels), jnp.float32))
    (sum_one, sum_two, sum_norms), features = lax.scan(per_clip, initial, (waveform, flat_lengths, cotangent))
    return (features, sum_one, sum_two, sum_norms)
```

```python
import functools

import jax
import jax.numpy as jnp
from jax import lax
from jax.experimental import pallas as pl
from jax.experimental.pallas import tpu as pltpu
from jax.sharding import PartitionSpec as P

MESH = pl.DeviceIdType.MESH
F32, BF16 = jnp.float32, jnp.bfloat16

epsilon = 1e-05
root_half = 0.7071067811865476
normal_peak = 0.3989422804014327

TAPS = 10
STEP = 32


def cdf(values):
    return 0.5 * (1.0 + lax.erf(values * root_half))


def slope_of(values, phi):
    return phi + values * jnp.exp(-0.5 * values * values) * normal_peak


def layer_norm(pre):
    centre = pre - jnp.mean(pre, axis=-1, keepdims=True)
    inverse = lax.rsqrt(jnp.mean(centre * centre, axis=-1, keepdims=True) + epsilon)
    return centre * inverse, inverse


def norm_backward(upstream, normed, inverse, gain):
    scaled = upstream * gain
    return inverse * (
        scaled
        - jnp.mean(scaled, axis=-1, keepdims=True)
        - normed * jnp.mean(scaled * normed, axis=-1, keepdims=True)
    )


def fold8(value):
    rows, channels = value.shape
    return jnp.sum(value.reshape(rows // 8, 8, channels), axis=0)


def dot_first(a, b):
    return lax.dot_general(a, b, (((0,), (0,)), ((), ())), preferred_element_type=F32)


def dot_last(a, b):
    return lax.dot_general(a, b, (((1,), (1,)), ((), ())), preferred_element_type=F32)


def kernel(
    ns, nz, parts, direct,
    wave_in, lengths_in, conv_one_in, conv_two_in, gain_one_in, shift_one_in, gain_two_in, shift_two_in, cot_in,
    features, grad_one_out, grad_two_out, norms_out,
    wave, lengths, conv_one, conv_two, gain_one, shift_one, gain_two, shift_two, cot, in_s,
    halo, patch, pre, hat, inv, phi, even, patch_two, pre_two, dpre_two, dpre_far, shifted, dact, dhi, dlo,
    order, cot_rows, feat, select,
    mine, from_seq, seq_sum, from_z, from_direct, full,
    small, small_core, small_sum, small_seq, small_part, small_z, small_all,
    halo_s, halo_r, p_s, p_r, a_s, a_r, b_s, b_r, c_s, c_r, d_s, d_r, e_s, e_r, f_s, f_r, g_s, g_r,
    sa_s, sa_r, sb_s, sb_r, sc_s, sc_r, sd_s, sd_r,
):
    clips, samples = wave.shape
    channels = conv_two.shape[1]
    half = samples // (2 * TAPS // 2)
    rows = clips * half
    middle = channels // 2
    block = mine.shape[1]
    body = rows - STEP

    pos = lax.axis_index("seq")
    dp = lax.axis_index("dp")
    z, core = dp // 2, lax.rem(dp, 2)
    partner = dp + 1 - 2 * core

    def at(dp_index, seq_index):
        return {"device_id": (dp_index, seq_index), "device_id_type": MESH}

    def seq_peer(d):
        return lax.rem(pos + d, ns)

    def z_peer(d):
        return lax.rem(z + d, nz)

    barrier = pltpu.get_barrier_semaphore()
    for d in range(1, nz):
        pl.semaphore_signal(barrier, inc=1, **at(2 * z_peer(d) + core, pos))
    for d in range(1, ns):
        pl.semaphore_signal(barrier, inc=1, **at(dp, seq_peer(d)))
    pl.semaphore_signal(barrier, inc=1, **at(partner, pos))
    loads = [
        pltpu.make_async_copy(source, target, in_s.at[i])
        for i, (source, target) in enumerate(
            (
                (wave_in, wave),
                (conv_one_in, conv_one),
                (gain_one_in, gain_one),
                (shift_one_in, shift_one),
                (lengths_in, lengths),
                (cot_in, cot),
                (gain_two_in, gain_two),
                (shift_two_in, shift_two),
                (conv_two_in, conv_two),
            )
        )
    ]
    for load in loads:
        load.start()

    def iota(shape, dim):
        return lax.broadcasted_iota(jnp.int32, shape, dim)

    for parity in range(2):
        tap = lax.rem(iota((samples, 128), 0) + (TAPS - parity * TAPS // 2), TAPS)
        select[parity] = jnp.where(tap == iota((samples, 128), 1), 1.0, 0.0).astype(BF16)

    for load in loads[:4]:
        load.wait()
    g1, b1 = gain_one[...], shift_one[...]
    taps = conv_one[...]
    wave_f = wave[...].astype(F32)
    spread = jnp.concatenate([wave_f] * (rows // clips), axis=0)
    lane = iota((rows, samples), 1) - TAPS * (iota((rows, samples), 0) // clips)
    for parity in range(2):
        offset = parity * TAPS // 2
        hit = (lane >= offset) & (lane < offset + TAPS)
        picked = jnp.where(hit, spread, 0.0).astype(BF16)
        found = jnp.dot(picked, select[parity], preferred_element_type=F32)
        patch[parity * rows : (parity + 1) * rows] = found
        pre[parity * rows : (parity + 1) * rows] = jnp.dot(
            found.astype(BF16)[:, 0:TAPS], taps, preferred_element_type=F32
        )

    def forward_one(value):
        normed, inverse = layer_norm(value)
        out = normed * g1 + b1
        probability = cdf(out)
        return normed, inverse, probability, out * probability

    def first_rows(r):
        normed, inverse, probability, act = forward_one(pre[pl.ds(r, STEP)])
        hat[pl.ds(r, STEP)] = normed
        inv[pl.ds(r, STEP)] = jnp.broadcast_to(inverse, (STEP, 128))
        phi[pl.ds(r, STEP)] = probability
        return act

    def even_rows(i):
        r = pl.multiple_of(i * STEP, STEP)
        act = first_rows(r)
        even[pl.ds(r, STEP)] = act
        patch_two[pl.ds(r, STEP), pl.ds(0, channels)] = act.astype(BF16)

    def odd_rows(i):
        r = pl.multiple_of(i * STEP, STEP)
        act = first_rows(pl.multiple_of(rows + r, STEP))
        patch_two[pl.ds(r, STEP), pl.ds(channels, channels)] = act.astype(BF16)

    blocks = rows // STEP
    pl.loop(0, blocks)(even_rows)
    pl.loop(0, blocks - 1)(odd_rows)

    pl.semaphore_wait(barrier, ns + nz - 1)
    halo_copy = pltpu.make_async_remote_copy(
        wave.at[:, pl.ds(0, 128)], halo, halo_s, halo_r, **at(dp, lax.rem(pos + ns - 1, ns))
    )
    halo_copy.start()

    patch_two[0:body, 2 * channels : 3 * channels] = even[clips : clips + body].astype(BF16)

    def patch_copy(which):
        start, count = ((0, body), (body, STEP))[which]
        return pltpu.make_async_remote_copy(
            patch_two.at[pl.ds(start, count)], patch_two.at[pl.ds(rows + start, count)],
            p_s.at[which], p_r.at[which], **at(partner, pos),
        )

    def dpre_copy(which):
        start, count = ((0, body), (body, STEP))[which]
        return pltpu.make_async_remote_copy(
            dpre_two.at[1 - core, pl.ds(start, count)], dpre_far.at[pl.ds(start, count)],
            a_s.at[which], a_r.at[which], **at(partner, pos),
        )

    patch_copy(0).start()

    for load in loads[4:6]:
        load.wait()
    clip_of = lax.rem(iota((rows, rows), 0), clips)
    frame_of = iota((rows, rows), 0) // clips
    limit = jnp.full((rows, rows), lengths[0, 0] // TAPS - 1, jnp.int32)
    for c in range(1, clips):
        limit = jnp.where(clip_of == c, lengths[0, c] // TAPS - 1, limit)
    order[...] = jnp.where(
        (iota((rows, rows), 1) == clip_of * half + frame_of) & (pos * half + frame_of < limit), 1.0, 0.0
    ).astype(BF16)
    cot_rows[...] = jnp.dot(order[...], cot[...], preferred_element_type=F32)

    for load in loads[6:]:
        load.wait()
    g2, b2 = gain_two[...], shift_two[...]
    pre_two[0:body] = jnp.dot(patch_two[0:body], conv_two[...], preferred_element_type=F32)

    zeros8 = jnp.zeros((8, channels), F32)

    def second(i, sums):
        r = pl.multiple_of(i * STEP, STEP)
        normed, inverse = layer_norm(pre_two[pl.ds(r, STEP)])
        out = normed * g2 + b2
        probability = cdf(out)
        feat[pl.ds(r, STEP)] = (out * probability).astype(BF16)
        up = cot_rows[pl.ds(r, STEP)] * slope_of(out, probability)
        down = norm_backward(up, normed, inverse, g2).astype(BF16)
        dpre_two[0, pl.ds(r, STEP)] = down[:, 0:middle]
        dpre_two[1, pl.ds(r, STEP)] = down[:, middle:channels]
        return sums[0] + fold8(up * normed), sums[1] + fold8(up)

    sums_two = lax.fori_loop(0, blocks - 1, second, (zeros8, zeros8))
    dpre_copy(0).start()

    inside = jnp.where(pos < ns - 1, 1.0, 0.0).astype(F32)
    taps_f = taps.astype(F32)
    late = jnp.concatenate([taps_f[TAPS // 2 : TAPS], jnp.zeros((TAPS // 2, channels), F32)], axis=0)
    both = jnp.concatenate([taps_f, late], axis=1).astype(BF16)
    halo_copy.wait()
    edge = (halo[...].astype(F32) * inside).astype(BF16)
    edges = jnp.dot(edge[:, 0:TAPS], both, preferred_element_type=F32)
    last = 2 * rows - clips
    pre[last : last + clips] = pre[last : last + clips] + edges[:, channels : 2 * channels]
    edge_hat, edge_inv, edge_phi, edge_act = forward_one(edges[:, 0:channels])
    even[rows : rows + clips] = edge_act * inside
    odd_rows(blocks - 1)
    patch_two[body:rows, 2 * channels : 3 * channels] = even[body + clips : rows + clips].astype(BF16)
    patch_copy(1).start()
    pre_two[body:rows] = jnp.dot(patch_two[body:rows], conv_two[...], preferred_element_type=F32)
    two_hat, two_up = second(blocks - 1, sums_two)
    dpre_copy(1).start()

    def back_dot(first):
        return dot_last(dpre_two[0], conv_two[first : first + channels, 0:middle]) + dot_last(
            dpre_two[1], conv_two[first : first + channels, middle:channels]
        )

    shifted[0:8] = jnp.zeros((8, channels), F32)
    shifted[8 : 8 + rows] = back_dot(2 * channels)
    dact[0:rows] = back_dot(0) + shifted[8 - clips : 8 - clips + rows]
    dact[rows : 2 * rows] = back_dot(channels)

    def seq_copy(q, d):
        start, count = parts[q]
        b = seq_peer(d)
        return pltpu.make_async_remote_copy(
            mine.at[b, pl.ds(start, count)], from_seq.at[d - 1, pl.ds(start, count)],
            b_s.at[q, d - 1], b_r.at[q, d - 1], **at(dp, b),
        )

    def pieces_of(q):
        return min(nz, parts[q][1] // 16)

    def z_rows(q, owner):
        piece = parts[q][1] // pieces_of(q)
        return pl.ds(pl.multiple_of(parts[q][0] + owner * piece, 16), piece)

    def z_copy(q, d):
        piece = parts[q][1] // pieces_of(q)
        return pltpu.make_async_remote_copy(
            seq_sum.at[z_rows(q, z_peer(d))], from_z.at[q, d - 1, pl.ds(0, piece)],
            c_s.at[q, d - 1], c_r.at[q, d - 1], **at(2 * z_peer(d) + core, pos),
        )

    def spread_copy(q, d):
        there = full.at[core, z_rows(q, z)]
        return pltpu.make_async_remote_copy(
            there, there, d_s.at[q, d - 1], d_r.at[q, d - 1], **at(2 * z_peer(d) + core, pos)
        )

    def spread_copy_from(q, d):
        there = full.at[core, z_rows(q, z_peer(nz - d))]
        return pltpu.make_async_remote_copy(
            there, there, d_s.at[q, d - 1], d_r.at[q, d - 1], **at(2 * z_peer(d) + core, pos)
        )

    def relay_copy(q, d, which):
        there = full.at[which, z_rows(q, z_peer(d))]
        return pltpu.make_async_remote_copy(
            there, there, e_s.at[q, d], e_r.at[q, d], **at(partner, pos)
        )

    def direct_rows(q):
        return pl.ds(parts[q][0], parts[q][1])

    def direct_copy(q, d):
        return pltpu.make_async_remote_copy(
            seq_sum.at[direct_rows(q)], from_direct.at[z], f_s.at[d - 1], f_r.at[d - 1],
            **at(2 * z_peer(d) + core, pos),
        )

    def direct_relay(q, which):
        there = full.at[which, direct_rows(q)]
        return pltpu.make_async_remote_copy(there, there, g_s, g_r, **at(partner, pos))

    def when_owner(q, owner, action):
        if pieces_of(q) == nz:
            action()
        else:
            pl.when(owner < pieces_of(q))(action)

    near = dpre_two[core]
    for which in range(2):
        patch_copy(which).wait_recv()
        dpre_copy(which).wait_recv()
    down = jnp.concatenate([near, dpre_far[...]], axis=0)
    if block % 128 == 0:
        for g in range(block // 128):
            for d in [*range(1, ns), 0]:
                b = seq_peer(d)
                columns = pl.ds(pl.multiple_of(b * block + g * 128, 128), 128)
                mine[b, g * 128 : (g + 1) * 128] = dot_first(patch_two[:, columns], down).astype(BF16)
                for q, (start, count) in enumerate(parts):
                    if d and g * 128 < start + count <= (g + 1) * 128:
                        seq_copy(q, d).start()
    else:
        group = 384
        for i in range(3 * channels // group):
            product = dot_first(patch_two[:, i * group : (i + 1) * group], down).astype(BF16)
            for j in range(group // block):
                mine[i * (group // block) + j] = product[j * block : (j + 1) * block]
        for q in range(len(parts)):
            for d in range(1, ns):
                seq_copy(q, d).start()

    def backward_one(incoming, normed, inverse, probability):
        up = incoming * slope_of(normed * g1 + b1, probability)
        return up, norm_backward(up, normed, inverse, g1)

    def back(i, sums):
        at_rows = pl.ds(pl.multiple_of(i * STEP, STEP), STEP)
        normed = hat[at_rows]
        up, dpre = backward_one(dact[at_rows], normed, inv[at_rows, 0:1], phi[at_rows])
        high = dpre.astype(BF16)
        dhi[at_rows] = high
        dlo[at_rows] = (dpre - high.astype(F32)).astype(BF16)
        return sums[0] + fold8(up * normed), sums[1] + fold8(up)

    one_hat, one_up = lax.fori_loop(0, 2 * rows // STEP, back, (zeros8, zeros8))

    edge_in = shifted[8 + rows - clips : 8 + rows] * inside
    edge_up, edge_dpre = backward_one(edge_in, edge_hat, edge_inv, edge_phi)
    edge_high = edge_dpre.astype(BF16)
    edge_low = (edge_dpre - edge_high.astype(F32)).astype(BF16)

    moved = iota((128, 128), 0) + TAPS // 2
    tap = iota((128, 128), 1)
    fix = jnp.dot(
        edge, jnp.where((moved == tap) & (tap < TAPS), 1.0, 0.0).astype(BF16), preferred_element_type=F32
    )
    patch[last : last + clips] = patch[last : last + clips] + fix
    frames = patch[...].astype(BF16)
    grad_one = (
        dot_first(frames, dhi[...])
        + dot_first(frames, dlo[...])
    )[0:16] + (dot_first(edge, edge_high) + dot_first(edge, edge_low))[0:16]

    def total_row(value):
        return jnp.sum(value, axis=0, keepdims=True)

    sums = (
        (0, grad_one),
        (10, total_row(one_hat) + total_row(edge_up * edge_hat)),
        (11, total_row(one_up) + total_row(edge_up)),
        (12, total_row(two_hat)),
        (13, total_row(two_up)),
        (14, jnp.zeros((2, channels), F32)),
    )
    for row, value in sums:
        for h in range(2):
            small[h, row : row + value.shape[0]] = value[:, h * middle : (h + 1) * middle]

    small_core_copy = pltpu.make_async_remote_copy(
        small.at[1 - core], small_core, sa_s, sa_r, **at(partner, pos)
    )
    small_core_copy.start()

    def small_seq_copy(d):
        return pltpu.make_async_remote_copy(
            small_sum, small_seq.at[pos], sb_s.at[d - 1], sb_r.at[d - 1], **at(dp, seq_peer(d))
        )

    def small_z_copy(d):
        return pltpu.make_async_remote_copy(
            small_part, small_z.at[z], sc_s.at[d - 1], sc_r.at[d - 1], **at(2 * z_peer(d) + core, pos)
        )

    def small_done_copy(which):
        return pltpu.make_async_remote_copy(
            small_all.at[which], small_all.at[which], sd_s, sd_r, **at(partner, pos)
        )

    def seq_done(q):
        span = pl.ds(parts[q][0], parts[q][1])
        total = mine[pos, span].astype(F32)
        for d in range(1, ns):
            seq_copy(q, d).wait_recv()
            total = total + from_seq[d - 1, span].astype(F32)
        value = total.astype(BF16)
        seq_sum[span] = value
        if q == direct:
            from_direct[z] = value
            for d in range(1, nz):
                direct_copy(q, d).start()
        else:
            for d in range(1, nz):
                when_owner(q, z_peer(d), lambda d=d: z_copy(q, d).start())

    def z_done(q):
        def action():
            piece = parts[q][1] // pieces_of(q)
            total = seq_sum[z_rows(q, z)].astype(F32)
            for d in range(1, nz):
                z_copy(q, d).wait_recv()
                total = total + from_z[q, d - 1, pl.ds(0, piece)].astype(F32)
            full[core, z_rows(q, z)] = total.astype(BF16)
            for d in range(1, nz):
                spread_copy(q, d).start()
            relay_copy(q, 0, core).start()

        when_owner(q, z, action)

    def direct_done(q):
        for d in range(1, nz):
            direct_copy(q, d).wait_recv()
        total = from_direct[0].astype(F32)
        for other in range(1, nz):
            total = total + from_direct[other].astype(F32)
        full[core, direct_rows(q)] = total.astype(BF16)
        direct_relay(q, core).start()

    def relay(q):
        for d in range(1, nz):
            def action(d=d):
                spread_copy_from(q, d).wait_recv()
                relay_copy(q, nz - d, core).start()

            when_owner(q, z_peer(nz - d), action)

    features[...] = dot_first(order[...], feat[...]).astype(BF16)

    def small_step(step):
        if step == 0:
            small_core_copy.wait()
            value = (small[core] + small_core[...]).astype(BF16)
            small_sum[...] = value
            small_seq[pos] = value
            for d in range(1, ns):
                small_seq_copy(d).start()
        elif step == 1:
            for d in range(1, ns):
                small_seq_copy(d).wait()
            total = small_seq[0].astype(F32)
            for p in range(1, ns):
                total = total + small_seq[p].astype(F32)
            value = total.astype(BF16)
            small_part[...] = value
            small_z[z] = value
            for d in range(1, nz):
                small_z_copy(d).start()
        else:
            for d in range(1, nz):
                small_z_copy(d).wait()
            total = small_z[0].astype(F32)
            for p in range(1, nz):
                total = total + small_z[p].astype(F32)
            small_all[core] = total
            small_done_copy(core).start()

    small_step(0)
    seq_done(0)
    seq_done(1)
    seq_done(2)
    z_done(0)
    seq_done(3)
    small_step(1)
    z_done(1)
    z_done(2)
    relay(0)
    small_step(2)
    relay(1)
    direct_done(direct)
    relay(2)

    small_done_copy(core).wait_send()
    small_done_copy(1 - core).wait_recv()
    for h in range(2):
        grad_one_out[:, h * middle : (h + 1) * middle] = small_all[h, 0:TAPS]
        norms_out[:, h * middle : (h + 1) * middle] = small_all[h, 10:14]

    for which in range(2):
        patch_copy(which).wait_send()
        dpre_copy(which).wait_send()
    for q in range(len(parts)):
        for d in range(1, ns):
            seq_copy(q, d).wait_send()
        if q == direct:
            for d in range(1, nz):
                direct_copy(q, d).wait_send()
            direct_relay(q, core).wait_send()
            direct_relay(q, 1 - core).wait_recv()
            continue
        for d in range(1, nz):
            when_owner(q, z_peer(d), lambda q=q, d=d: z_copy(q, d).wait_send())

        def sent(q=q):
            for d in range(1, nz):
                spread_copy(q, d).wait_send()

        when_owner(q, z, sent)
        for d in range(nz):

            def relayed(q=q, d=d):
                relay_copy(q, d, core).wait_send()
                relay_copy(q, d, 1 - core).wait_recv()

            when_owner(q, z_peer(d), relayed)
    for h in range(2):
        grad_two_out[:, h * middle : (h + 1) * middle] = full[h]


def on_device(ns, nz, waveform, lengths, conv_one, conv_two, gain_one, shift_one, gain_two, shift_two, cotangent):
    clips, samples = waveform.shape
    channels = conv_two.shape[1]
    half = cotangent.shape[1]
    rows = clips * half
    block = conv_two.shape[0] // ns
    unit = block // 6
    parts = ((0, 2 * unit), (2 * unit, 2 * unit), (4 * unit, unit), (5 * unit, unit))
    direct = len(parts) - 1
    count = len(parts)
    piece = max(size // min(nz, size // 16) for _, size in parts[:direct])
    middle = channels // 2
    dma = pltpu.SemaphoreType.DMA
    vmem = pl.BlockSpec(memory_space=pltpu.VMEM)
    hbm = pl.BlockSpec(memory_space=pltpu.HBM)
    features, grad_one, grad_two, norms = pl.pallas_call(
        functools.partial(kernel, ns, nz, parts, direct),
        out_shape=(
            jax.ShapeDtypeStruct((rows, channels), BF16),
            jax.ShapeDtypeStruct((TAPS, channels), F32),
            jax.ShapeDtypeStruct((block, channels), BF16),
            jax.ShapeDtypeStruct((4, channels), F32),
        ),
        in_specs=[hbm] * 9,
        out_specs=(vmem,) * 4,
        scratch_shapes=[
            pltpu.VMEM(waveform.shape, BF16),
            pltpu.SMEM(lengths.shape, jnp.int32),
            pltpu.VMEM(conv_one.shape, BF16),
            pltpu.VMEM(conv_two.shape, BF16),
            pltpu.VMEM((1, channels), F32),
            pltpu.VMEM((1, channels), F32),
            pltpu.VMEM((1, channels), F32),
            pltpu.VMEM((1, channels), F32),
            pltpu.VMEM((rows, channels), BF16),
            dma((9,)),
            pltpu.VMEM((clips, 128), BF16),
            pltpu.VMEM((2 * rows, 128), F32),
            pltpu.VMEM((2 * rows, channels), F32),
            pltpu.VMEM((2 * rows, channels), F32),
            pltpu.VMEM((2 * rows, 128), F32),
            pltpu.VMEM((2 * rows, channels), F32),
            pltpu.VMEM((rows + 8, channels), F32),
            pltpu.VMEM((2 * rows, 3 * channels), BF16),
            pltpu.VMEM((rows, channels), F32),
            pltpu.VMEM((2, rows, middle), BF16),
            pltpu.VMEM((rows, middle), BF16),
            pltpu.VMEM((rows + 8, channels), F32),
            pltpu.VMEM((2 * rows, channels), F32),
            pltpu.VMEM((2 * rows, channels), BF16),
            pltpu.VMEM((2 * rows, channels), BF16),
            pltpu.VMEM((rows, rows), BF16),
            pltpu.VMEM((rows, channels), F32),
            pltpu.VMEM((rows, channels), BF16),
            pltpu.VMEM((2, samples, 128), BF16),
            pltpu.VMEM((ns, block, middle), BF16),
            pltpu.VMEM((ns - 1, block, middle), BF16),
            pltpu.VMEM((block, middle), BF16),
            pltpu.VMEM((direct, nz - 1, piece, middle), BF16),
            pltpu.VMEM((nz, parts[direct][1], middle), BF16),
            pltpu.VMEM((2, block, middle), BF16),
            pltpu.VMEM((2, 16, middle), F32),
            pltpu.VMEM((16, middle), F32),
            pltpu.VMEM((16, middle), BF16),
            pltpu.VMEM((ns, 16, middle), BF16),
            pltpu.VMEM((16, middle), BF16),
            pltpu.VMEM((nz, 16, middle), BF16),
            pltpu.VMEM((2, 16, middle), F32),
            dma, dma,
            dma((2,)), dma((2,)),
            dma((2,)), dma((2,)),
            dma((count, ns - 1)), dma((count, ns - 1)),
            dma((count, nz - 1)), dma((count, nz - 1)),
            dma((count, nz - 1)), dma((count, nz - 1)),
            dma((count, nz)), dma((count, nz)),
            dma((nz - 1,)), dma((nz - 1,)),
            dma, dma,
            dma, dma,
            dma((ns - 1,)), dma((ns - 1,)),
            dma((nz - 1,)), dma((nz - 1,)),
            dma, dma,
        ],
        compiler_params=pltpu.CompilerParams(
            collective_id=0, has_side_effects=True, vmem_limit_bytes=48 * 1024 * 1024
        ),
    )(
        *[
            pltpu.with_memory_space_constraint(value, pltpu.HBM)
            for value in (
        waveform,
        lengths,
        conv_one,
        conv_two,
        gain_one.reshape(1, channels),
        shift_one.reshape(1, channels),
        gain_two.reshape(1, channels),
        shift_two.reshape(1, channels),
        cotangent.reshape(rows, channels),
    )])
    features, grad_one, grad_two, norms = pl.pallas_call(
        put_out,
        out_shape=(
            jax.ShapeDtypeStruct((rows, channels), BF16),
            jax.ShapeDtypeStruct((TAPS, channels), F32),
            jax.ShapeDtypeStruct((block, channels), F32),
            jax.ShapeDtypeStruct((4, channels), F32),
        ),
        in_specs=[vmem] * 4,
        out_specs=(hbm,) * 4,
        scratch_shapes=[pltpu.VMEM((block, channels), F32), dma((4,))],
        compiler_params=pltpu.CompilerParams(vmem_limit_bytes=4 * 1024 * 1024),
    )(features, grad_one, grad_two, norms)
    return features.reshape(clips, half, channels), grad_one, grad_two, norms


def put_out(features, grad_one, grad_two, norms, features_out, grad_one_out, grad_two_out, norms_out, wide, sem):
    copies = [
        pltpu.make_async_copy(source, target, sem.at[i])
        for i, (source, target) in enumerate(
            (
                (features, features_out),
                (grad_one, grad_one_out),
                (norms, norms_out),
                (wide, grad_two_out),
            )
        )
    ]
    for copy in copies[:3]:
        copy.start()
    wide[...] = grad_two[...].astype(F32)
    copies[3].start()
    for copy in copies:
        copy.wait()


def solution(mesh):
    in_specs = (P("dp", "seq"), P("dp", None), P(), P(), P(), P(), P(), P(), P("dp", "seq", None))
    out_specs = (P("dp", "seq", None), P(), P("seq", None), P())
    return jax.shard_map(
        functools.partial(on_device, mesh.shape["seq"], mesh.shape["dp"] // 2),
        mesh=mesh, in_specs=in_specs, out_specs=out_specs, check_vma=False,
    )
```

```python
import functools

import jax
import jax.numpy as jnp
from jax import lax
from jax.experimental import pallas as pl
from jax.experimental.pallas import tpu as pltpu
from jax.sharding import PartitionSpec as P

MESH = pl.DeviceIdType.MESH
F32, BF16 = jnp.float32, jnp.bfloat16

epsilon = 1e-05
root_half = 0.7071067811865476
normal_peak = 0.3989422804014327

TAPS = 10
STEP = 16
UNROLL = 8


def half_erfc_terms():
    scaled = (0.254829592, -0.284496736, 1.421413741, -1.453152027, 1.061405429)
    return [0.5 * term for term in scaled]


def cdf_and_bell(values):
    t = pltpu.reciprocal(1.0 + 0.3275911 * root_half * jnp.abs(values), approx=True)
    bell = jnp.exp(-0.5 * values * values)
    c1, c2, c3, c4, c5 = half_erfc_terms()
    tail = t * (c1 + t * (c2 + t * (c3 + t * (c4 + t * c5)))) * bell
    return jnp.where(values >= 0.0, 1.0 - tail, tail), bell


def slope_of(values, phi):
    return phi + values * jnp.exp(-0.5 * values * values) * normal_peak


def scale_norm(centre):
    inverse = lax.rsqrt(jnp.mean(centre * centre, axis=-1, keepdims=True) + epsilon)
    return centre * inverse, inverse


def layer_norm(pre):
    return scale_norm(pre - jnp.mean(pre, axis=-1, keepdims=True))


def norm_backward(upstream, normed, inverse, gain):
    scaled = upstream * gain
    return inverse * (
        scaled
        - jnp.mean(scaled, axis=-1, keepdims=True)
        - normed * jnp.mean(scaled * normed, axis=-1, keepdims=True)
    )


def fold8(value):
    rows, channels = value.shape
    return jnp.sum(value.reshape(rows // 8, 8, channels), axis=0)


def dot_first(a, b):
    return lax.dot_general(a, b, (((0,), (0,)), ((), ())), preferred_element_type=F32)


def dot_last(a, b):
    return lax.dot_general(a, b, (((1,), (1,)), ((), ())), preferred_element_type=F32)


def kernel(
    ns, nz, parts, direct,
    wave_in, lengths_in, conv_one_in, conv_two_in, gain_one_in, shift_one_in, gain_two_in, shift_two_in, cot_in,
    features, grad_one_out, grad_two_out, norms_out,
    wave, lengths, conv_one, conv_two, gain_one, shift_one, gain_two, shift_two, cot, in_s,
    halo, patch, pre, hat, inv, phi, even, patch_two, pre_two, dpre_two, dpre_far, shifted, dact, dhi, dlo,
    order, cot_rows, feat, select,
    mine, from_seq, seq_sum, from_z, from_direct, full,
    small, small_core, small_sum, small_seq, small_part, small_z, small_all,
    halo_s, halo_r, p_s, p_r, a_s, a_r, b_s, b_r, c_s, c_r, d_s, d_r, e_s, e_r, f_s, f_r, g_s, g_r,
    sa_s, sa_r, sb_s, sb_r, sc_s, sc_r, sd_s, sd_r,
):
    clips, samples = wave.shape
    channels = conv_two.shape[1]
    half = samples // (2 * TAPS // 2)
    rows = clips * half
    middle = channels // 2
    block = mine.shape[1]

    pos = lax.axis_index("seq")
    dp = lax.axis_index("dp")
    z, core = dp // 2, lax.rem(dp, 2)
    partner = dp + 1 - 2 * core

    def at(dp_index, seq_index):
        return {"device_id": (dp_index, seq_index), "device_id_type": MESH}

    def seq_peer(d):
        return lax.rem(pos + d, ns)

    def z_peer(d):
        return lax.rem(z + d, nz)

    loads = [
        pltpu.make_async_copy(source, target, in_s.at[i])
        for i, (source, target) in enumerate(
            (
                (wave_in, wave),
                (conv_one_in, conv_one),
                (gain_one_in, gain_one),
                (shift_one_in, shift_one),
                (lengths_in, lengths),
                (cot_in, cot),
                (gain_two_in, gain_two),
                (shift_two_in, shift_two),
                (conv_two_in, conv_two),
            )
        )
    ]
    for load in loads[:4]:
        load.start()
    barrier = pltpu.get_barrier_semaphore()
    for d in range(1, nz):
        pl.semaphore_signal(barrier, inc=1, **at(2 * z_peer(d) + core, pos))
    for d in range(1, ns):
        pl.semaphore_signal(barrier, inc=1, **at(dp, seq_peer(d)))
    pl.semaphore_signal(barrier, inc=1, **at(partner, pos))
    for load in loads[4:]:
        load.start()

    def iota(shape, dim):
        return lax.broadcasted_iota(jnp.int32, shape, dim)

    for parity in range(2):
        tap = lax.rem(iota((samples, 128), 0) + (TAPS - parity * TAPS // 2), TAPS)
        column = iota((samples, 128), 1)
        select[parity] = jnp.where(
            (tap == lax.rem(column, TAPS)) & (column < 3 * TAPS), 1.0, 0.0
        ).astype(BF16)

    for load in loads[:4]:
        load.wait()
    g1, b1 = gain_one[...], shift_one[...]
    taps = conv_one[...].astype(F32)
    taps = taps - jnp.mean(taps, axis=-1, keepdims=True)
    high = taps.astype(BF16).astype(F32)
    middling = (taps - high).astype(BF16).astype(F32)
    low = taps - high - middling
    thirds = jnp.concatenate([high, middling, low], axis=0).astype(BF16)
    wave_f = wave[...].astype(F32)
    spread = jnp.concatenate([wave_f] * (rows // clips), axis=0)
    lane = iota((rows, samples), 1) - TAPS * (iota((rows, samples), 0) // clips)
    for parity in range(2):
        offset = parity * TAPS // 2
        hit = (lane >= offset) & (lane < offset + TAPS)
        picked = jnp.where(hit, spread, 0.0).astype(BF16)
        found = jnp.dot(picked, select[parity], preferred_element_type=F32)
        patch[parity * rows : (parity + 1) * rows] = found
        pre[parity * rows : (parity + 1) * rows] = jnp.dot(
            found.astype(BF16)[:, 0 : 3 * TAPS], thirds, preferred_element_type=F32
        )

    pl.semaphore_wait(barrier, ns + nz - 1)
    halo_copy = pltpu.make_async_remote_copy(
        wave.at[:, pl.ds(0, 128)], halo, halo_s, halo_r, **at(dp, lax.rem(pos + ns - 1, ns))
    )
    halo_copy.start()

    def forward_one(value):
        normed, inverse = scale_norm(value)
        out = normed * g1 + b1
        probability, _ = cdf_and_bell(out)
        return normed, inverse, probability, out * probability

    def first_rows(r):
        normed, inverse, probability, act = forward_one(pre[pl.ds(r, STEP)])
        hat[pl.ds(r, STEP)] = normed
        inv[pl.ds(r, STEP)] = jnp.broadcast_to(inverse, (STEP, 128))
        phi[pl.ds(r, STEP)] = probability
        return act

    def even_rows(i):
        r = pl.multiple_of(i * STEP, STEP)
        act = first_rows(r)
        even[pl.ds(r, STEP)] = act
        patch_two[pl.ds(r, STEP), pl.ds(0, channels)] = act.astype(BF16)

    def odd_rows(i):
        r = pl.multiple_of(i * STEP, STEP)
        act = first_rows(pl.multiple_of(rows + r, STEP))
        patch_two[pl.ds(r, STEP), pl.ds(channels, channels)] = act.astype(BF16)

    blocks = rows // STEP
    pl.loop(0, blocks, unroll=UNROLL)(even_rows)
    pl.loop(0, blocks - 1, unroll=UNROLL)(odd_rows)

    inside = jnp.where(pos < ns - 1, 1.0, 0.0).astype(F32)
    halo_copy.wait_recv()
    edge = (halo[...].astype(F32) * inside).astype(BF16)
    moved = iota((128, 128), 0) + TAPS // 2
    tap = iota((128, 128), 1)
    fix = jnp.dot(
        edge,
        jnp.where((moved == lax.rem(tap, TAPS)) & (tap < 3 * TAPS), 1.0, 0.0).astype(BF16),
        preferred_element_type=F32,
    )
    three = iota((128, 128), 0) == lax.rem(tap, TAPS)
    tripled = jnp.dot(
        edge, jnp.where(three & (tap < 3 * TAPS), 1.0, 0.0).astype(BF16), preferred_element_type=F32
    )
    last = 2 * rows - clips
    patch[last : last + clips] = patch[last : last + clips] + fix
    fix_pre = jnp.dot(fix.astype(BF16)[:, 0 : 3 * TAPS], thirds, preferred_element_type=F32)
    edge_pre = jnp.dot(tripled.astype(BF16)[:, 0 : 3 * TAPS], thirds, preferred_element_type=F32)
    pre[last : last + clips] = pre[last : last + clips] + fix_pre
    edge_hat, edge_inv, edge_phi, edge_act = forward_one(edge_pre)
    even[rows : rows + clips] = edge_act * inside
    odd_rows(blocks - 1)
    patch_two[0:rows, 2 * channels : 3 * channels] = even[clips : clips + rows].astype(BF16)
    patch_copy = pltpu.make_async_remote_copy(
        patch_two.at[pl.ds(0, rows)], patch_two.at[pl.ds(rows, rows)], p_s, p_r, **at(partner, pos)
    )

    def dpre_copy(which):
        part = pl.ds(which * (rows // 2), rows // 2)
        return pltpu.make_async_remote_copy(
            dpre_two.at[1 - core, part], dpre_far.at[part], a_s.at[which], a_r.at[which], **at(partner, pos)
        )

    patch_copy.start()

    for load in loads[4:6]:
        load.wait()
    clip_of = lax.rem(iota((rows, rows), 0), clips)
    frame_of = iota((rows, rows), 0) // clips
    limit = jnp.full((rows, rows), lengths[0, 0] // TAPS - 1, jnp.int32)
    for c in range(1, clips):
        limit = jnp.where(clip_of == c, lengths[0, c] // TAPS - 1, limit)
    order[...] = jnp.where(
        (iota((rows, rows), 1) == clip_of * half + frame_of) & (pos * half + frame_of < limit), 1.0, 0.0
    ).astype(BF16)
    cot_rows[...] = jnp.dot(order[...], cot[...], preferred_element_type=F32)

    for load in loads[6:]:
        load.wait()
    g2, b2 = gain_two[...], shift_two[...]
    pre_two[...] = jnp.dot(patch_two[0:rows], conv_two[...], preferred_element_type=F32)

    zeros8 = jnp.zeros((8, channels), F32)

    def second(i, sums):
        r = pl.multiple_of(i * STEP, STEP)
        normed, inverse = layer_norm(pre_two[pl.ds(r, STEP)])
        out = normed * g2 + b2
        probability, bell = cdf_and_bell(out)
        feat[pl.ds(r, STEP)] = (out * probability).astype(BF16)
        up = cot_rows[pl.ds(r, STEP)] * (probability + out * bell * normal_peak)
        down = norm_backward(up, normed, inverse, g2).astype(BF16)
        dpre_two[0, pl.ds(r, STEP)] = down[:, 0:middle]
        dpre_two[1, pl.ds(r, STEP)] = down[:, middle:channels]
        return sums[0] + fold8(up * normed), sums[1] + fold8(up)

    sums_two = lax.fori_loop(0, blocks // 2, second, (zeros8, zeros8), unroll=UNROLL)
    dpre_copy(0).start()
    two_hat, two_up = lax.fori_loop(blocks // 2, blocks, second, sums_two, unroll=UNROLL)
    dpre_copy(1).start()

    def back_dot(first):
        return dot_last(dpre_two[0], conv_two[first : first + channels, 0:middle]) + dot_last(
            dpre_two[1], conv_two[first : first + channels, middle:channels]
        )

    shifted[0:8] = jnp.zeros((8, channels), F32)
    shifted[8 : 8 + rows] = back_dot(2 * channels)
    dact[0:rows] = back_dot(0) + shifted[8 - clips : 8 - clips + rows]
    dact[rows : 2 * rows] = back_dot(channels)

    def seq_copy(q, d):
        start, count = parts[q]
        b = seq_peer(d)
        return pltpu.make_async_remote_copy(
            mine.at[b, pl.ds(start, count)], from_seq.at[d - 1, pl.ds(start, count)],
            b_s.at[q, d - 1], b_r.at[q, d - 1], **at(dp, b),
        )

    def pieces_of(q):
        return min(nz, parts[q][1] // 16)

    def z_rows(q, owner):
        piece = parts[q][1] // pieces_of(q)
        return pl.ds(pl.multiple_of(parts[q][0] + owner * piece, 16), piece)

    def z_copy(q, d):
        piece = parts[q][1] // pieces_of(q)
        return pltpu.make_async_remote_copy(
            seq_sum.at[z_rows(q, z_peer(d))], from_z.at[q, d - 1, pl.ds(0, piece)],
            c_s.at[q, d - 1], c_r.at[q, d - 1], **at(2 * z_peer(d) + core, pos),
        )

    def spread_copy(q, d):
        there = full.at[core, z_rows(q, z)]
        return pltpu.make_async_remote_copy(
            there, there, d_s.at[q, d - 1], d_r.at[q, d - 1], **at(2 * z_peer(d) + core, pos)
        )

    def spread_copy_from(q, d):
        there = full.at[core, z_rows(q, z_peer(nz - d))]
        return pltpu.make_async_remote_copy(
            there, there, d_s.at[q, d - 1], d_r.at[q, d - 1], **at(2 * z_peer(d) + core, pos)
        )

    def relay_copy(q, d, which):
        there = full.at[which, z_rows(q, z_peer(d))]
        return pltpu.make_async_remote_copy(
            there, there, e_s.at[q, d], e_r.at[q, d], **at(partner, pos)
        )

    def direct_rows(q):
        return pl.ds(parts[q][0], parts[q][1])

    def direct_copy(q, d):
        return pltpu.make_async_remote_copy(
            seq_sum.at[direct_rows(q)], from_direct.at[z], f_s.at[d - 1], f_r.at[d - 1],
            **at(2 * z_peer(d) + core, pos),
        )

    def direct_relay(q, which):
        there = full.at[which, direct_rows(q)]
        return pltpu.make_async_remote_copy(there, there, g_s, g_r, **at(partner, pos))

    def when_owner(q, owner, action):
        if pieces_of(q) == nz:
            action()
        else:
            pl.when(owner < pieces_of(q))(action)

    near = dpre_two[core]
    patch_copy.wait_recv()
    for which in range(2):
        dpre_copy(which).wait_recv()
    down = jnp.concatenate([near, dpre_far[...]], axis=0)
    if block % 128 == 0:
        for g in range(block // 128):
            for d in [*range(1, ns), 0]:
                b = seq_peer(d)
                columns = pl.ds(pl.multiple_of(b * block + g * 128, 128), 128)
                mine[b, g * 128 : (g + 1) * 128] = dot_first(patch_two[:, columns], down).astype(BF16)
                for q, (start, count) in enumerate(parts):
                    if d and g * 128 < start + count <= (g + 1) * 128:
                        seq_copy(q, d).start()
    else:
        group = 384
        for i in range(3 * channels // group):
            product = dot_first(patch_two[:, i * group : (i + 1) * group], down).astype(BF16)
            for j in range(group // block):
                mine[i * (group // block) + j] = product[j * block : (j + 1) * block]
        for q in range(len(parts)):
            for d in range(1, ns):
                seq_copy(q, d).start()

    def backward_one(incoming, normed, inverse, probability):
        up = incoming * slope_of(normed * g1 + b1, probability)
        return up, norm_backward(up, normed, inverse, g1)

    def back(i, sums):
        at_rows = pl.ds(pl.multiple_of(i * STEP, STEP), STEP)
        normed = hat[at_rows]
        up, dpre = backward_one(dact[at_rows], normed, inv[at_rows, 0:1], phi[at_rows])
        high = dpre.astype(BF16)
        dhi[at_rows] = high
        dlo[at_rows] = (dpre - high.astype(F32)).astype(BF16)
        return sums[0] + fold8(up * normed), sums[1] + fold8(up)

    one_hat, one_up = lax.fori_loop(0, 2 * rows // STEP, back, (zeros8, zeros8), unroll=UNROLL)

    edge_in = shifted[8 + rows - clips : 8 + rows] * inside
    edge_up, edge_dpre = backward_one(edge_in, edge_hat, edge_inv, edge_phi)
    edge_high = edge_dpre.astype(BF16)
    edge_low = (edge_dpre - edge_high.astype(F32)).astype(BF16)

    frames = patch[...].astype(BF16)
    grad_one = (
        dot_first(frames, dhi[...])
        + dot_first(frames, dlo[...])
    )[0:16] + (dot_first(edge, edge_high) + dot_first(edge, edge_low))[0:16]

    def total_row(value):
        return jnp.sum(value, axis=0, keepdims=True)

    sums = (
        (0, grad_one),
        (10, total_row(one_hat) + total_row(edge_up * edge_hat)),
        (11, total_row(one_up) + total_row(edge_up)),
        (12, total_row(two_hat)),
        (13, total_row(two_up)),
        (14, jnp.zeros((2, channels), F32)),
    )
    for row, value in sums:
        for h in range(2):
            small[h, row : row + value.shape[0]] = value[:, h * middle : (h + 1) * middle]

    small_core_copy = pltpu.make_async_remote_copy(
        small.at[1 - core], small_core, sa_s, sa_r, **at(partner, pos)
    )
    small_core_copy.start()

    def small_seq_copy(d):
        return pltpu.make_async_remote_copy(
            small_sum, small_seq.at[pos], sb_s.at[d - 1], sb_r.at[d - 1], **at(dp, seq_peer(d))
        )

    def small_z_copy(d):
        return pltpu.make_async_remote_copy(
            small_part, small_z.at[z], sc_s.at[d - 1], sc_r.at[d - 1], **at(2 * z_peer(d) + core, pos)
        )

    def small_done_copy(which):
        return pltpu.make_async_remote_copy(
            small_all.at[which], small_all.at[which], sd_s, sd_r, **at(partner, pos)
        )

    def seq_done(q):
        span = pl.ds(parts[q][0], parts[q][1])
        total = mine[pos, span].astype(F32)
        for d in range(1, ns):
            seq_copy(q, d).wait_recv()
            total = total + from_seq[d - 1, span].astype(F32)
        value = total.astype(BF16)
        seq_sum[span] = value
        if q == direct:
            from_direct[z] = value
            for d in range(1, nz):
                direct_copy(q, d).start()
        else:
            for d in range(1, nz):
                when_owner(q, z_peer(d), lambda d=d: z_copy(q, d).start())

    def z_done(q):
        def action():
            piece = parts[q][1] // pieces_of(q)
            total = seq_sum[z_rows(q, z)].astype(F32)
            for d in range(1, nz):
                z_copy(q, d).wait_recv()
                total = total + from_z[q, d - 1, pl.ds(0, piece)].astype(F32)
            full[core, z_rows(q, z)] = total.astype(BF16)
            for d in range(1, nz):
                spread_copy(q, d).start()
            relay_copy(q, 0, core).start()

        when_owner(q, z, action)

    def direct_done(q):
        for d in range(1, nz):
            direct_copy(q, d).wait_recv()
        total = from_direct[0].astype(F32)
        for other in range(1, nz):
            total = total + from_direct[other].astype(F32)
        full[core, direct_rows(q)] = total.astype(BF16)
        direct_relay(q, core).start()

    def relay(q):
        for d in range(1, nz):
            def action(d=d):
                spread_copy_from(q, d).wait_recv()
                relay_copy(q, nz - d, core).start()

            when_owner(q, z_peer(nz - d), action)

    features[...] = dot_first(order[...], feat[...]).astype(BF16)

    def small_step(step):
        if step == 0:
            small_core_copy.wait_recv()
            value = (small[core] + small_core[...]).astype(BF16)
            small_part[...] = value
            small_z[z] = value
            for d in range(1, nz):
                small_z_copy(d).start()
        elif step == 1:
            for d in range(1, nz):
                small_z_copy(d).wait_recv()
            total = small_z[0].astype(F32)
            for p in range(1, nz):
                total = total + small_z[p].astype(F32)
            value = total.astype(BF16)
            small_sum[...] = value
            small_seq[pos] = value
            for d in range(1, ns):
                small_seq_copy(d).start()
        else:
            for d in range(1, ns):
                small_seq_copy(d).wait_recv()
            total = small_seq[0].astype(F32)
            for p in range(1, ns):
                total = total + small_seq[p].astype(F32)
            small_all[core] = total
            small_done_copy(core).start()

    small_step(0)
    seq_done(0)
    seq_done(1)
    small_step(1)
    seq_done(2)
    z_done(0)
    seq_done(3)
    z_done(1)
    z_done(2)
    relay(0)
    small_step(2)
    relay(1)
    direct_done(direct)
    relay(2)

    small_done_copy(core).wait_send()
    small_done_copy(1 - core).wait_recv()
    for h in range(2):
        grad_one_out[:, h * middle : (h + 1) * middle] = small_all[h, 0:TAPS]
        norms_out[:, h * middle : (h + 1) * middle] = small_all[h, 10:14]

    small_core_copy.wait_send()
    for d in range(1, nz):
        small_z_copy(d).wait_send()
    for d in range(1, ns):
        small_seq_copy(d).wait_send()
    halo_copy.wait_send()
    patch_copy.wait_send()
    for which in range(2):
        dpre_copy(which).wait_send()
    for q in range(len(parts)):
        for d in range(1, ns):
            seq_copy(q, d).wait_send()
        if q == direct:
            for d in range(1, nz):
                direct_copy(q, d).wait_send()
            direct_relay(q, core).wait_send()
            direct_relay(q, 1 - core).wait_recv()
            continue
        for d in range(1, nz):
            when_owner(q, z_peer(d), lambda q=q, d=d: z_copy(q, d).wait_send())

        def sent(q=q):
            for d in range(1, nz):
                spread_copy(q, d).wait_send()

        when_owner(q, z, sent)
        for d in range(nz):

            def relayed(q=q, d=d):
                relay_copy(q, d, core).wait_send()
                relay_copy(q, d, 1 - core).wait_recv()

            when_owner(q, z_peer(d), relayed)
    for h in range(2):
        grad_two_out[:, h * middle : (h + 1) * middle] = full[h]


def on_device(ns, nz, waveform, lengths, conv_one, conv_two, gain_one, shift_one, gain_two, shift_two, cotangent):
    clips, samples = waveform.shape
    channels = conv_two.shape[1]
    half = cotangent.shape[1]
    rows = clips * half
    block = conv_two.shape[0] // ns
    unit = block // 6
    parts = ((0, 2 * unit), (2 * unit, 2 * unit), (4 * unit, unit), (5 * unit, unit))
    direct = len(parts) - 1
    count = len(parts)
    piece = max(size // min(nz, size // 16) for _, size in parts[:direct])
    middle = channels // 2
    dma = pltpu.SemaphoreType.DMA
    vmem = pl.BlockSpec(memory_space=pltpu.VMEM)
    hbm = pl.BlockSpec(memory_space=pltpu.HBM)
    features, grad_one, grad_two, norms = pl.pallas_call(
        functools.partial(kernel, ns, nz, parts, direct),
        out_shape=(
            jax.ShapeDtypeStruct((rows, channels), BF16),
            jax.ShapeDtypeStruct((TAPS, channels), F32),
            jax.ShapeDtypeStruct((block, channels), BF16),
            jax.ShapeDtypeStruct((4, channels), F32),
        ),
        in_specs=[hbm] * 9,
        out_specs=(vmem,) * 4,
        scratch_shapes=[
            pltpu.VMEM(waveform.shape, BF16),
            pltpu.SMEM(lengths.shape, jnp.int32),
            pltpu.VMEM(conv_one.shape, BF16),
            pltpu.VMEM(conv_two.shape, BF16),
            pltpu.VMEM((1, channels), F32),
            pltpu.VMEM((1, channels), F32),
            pltpu.VMEM((1, channels), F32),
            pltpu.VMEM((1, channels), F32),
            pltpu.VMEM((rows, channels), BF16),
            dma((9,)),
            pltpu.VMEM((clips, 128), BF16),
            pltpu.VMEM((2 * rows, 128), F32),
            pltpu.VMEM((2 * rows, channels), F32),
            pltpu.VMEM((2 * rows, channels), F32),
            pltpu.VMEM((2 * rows, 128), F32),
            pltpu.VMEM((2 * rows, channels), F32),
            pltpu.VMEM((rows + 8, channels), F32),
            pltpu.VMEM((2 * rows, 3 * channels), BF16),
            pltpu.VMEM((rows, channels), F32),
            pltpu.VMEM((2, rows, middle), BF16),
            pltpu.VMEM((rows, middle), BF16),
            pltpu.VMEM((rows + 8, channels), F32),
            pltpu.VMEM((2 * rows, channels), F32),
            pltpu.VMEM((2 * rows, channels), BF16),
            pltpu.VMEM((2 * rows, channels), BF16),
            pltpu.VMEM((rows, rows), BF16),
            pltpu.VMEM((rows, channels), F32),
            pltpu.VMEM((rows, channels), BF16),
            pltpu.VMEM((2, samples, 128), BF16),
            pltpu.VMEM((ns, block, middle), BF16),
            pltpu.VMEM((ns - 1, block, middle), BF16),
            pltpu.VMEM((block, middle), BF16),
            pltpu.VMEM((direct, nz - 1, piece, middle), BF16),
            pltpu.VMEM((nz, parts[direct][1], middle), BF16),
            pltpu.VMEM((2, block, middle), BF16),
            pltpu.VMEM((2, 16, middle), F32),
            pltpu.VMEM((16, middle), F32),
            pltpu.VMEM((16, middle), BF16),
            pltpu.VMEM((ns, 16, middle), BF16),
            pltpu.VMEM((16, middle), BF16),
            pltpu.VMEM((nz, 16, middle), BF16),
            pltpu.VMEM((2, 16, middle), F32),
            dma, dma,
            dma, dma,
            dma((2,)), dma((2,)),
            dma((count, ns - 1)), dma((count, ns - 1)),
            dma((count, nz - 1)), dma((count, nz - 1)),
            dma((count, nz - 1)), dma((count, nz - 1)),
            dma((count, nz)), dma((count, nz)),
            dma((nz - 1,)), dma((nz - 1,)),
            dma, dma,
            dma, dma,
            dma((ns - 1,)), dma((ns - 1,)),
            dma((nz - 1,)), dma((nz - 1,)),
            dma, dma,
        ],
        compiler_params=pltpu.CompilerParams(
            collective_id=0, has_side_effects=True, vmem_limit_bytes=48 * 1024 * 1024
        ),
    )(
        *[
            pltpu.with_memory_space_constraint(value, pltpu.HBM)
            for value in (
        waveform,
        lengths,
        conv_one,
        conv_two,
        gain_one.reshape(1, channels),
        shift_one.reshape(1, channels),
        gain_two.reshape(1, channels),
        shift_two.reshape(1, channels),
        cotangent.reshape(rows, channels),
    )])
    features, grad_one, grad_two, norms = pl.pallas_call(
        put_out,
        out_shape=(
            jax.ShapeDtypeStruct((rows, channels), BF16),
            jax.ShapeDtypeStruct((TAPS, channels), F32),
            jax.ShapeDtypeStruct((block, channels), F32),
            jax.ShapeDtypeStruct((4, channels), F32),
        ),
        in_specs=[vmem] * 4,
        out_specs=(hbm,) * 4,
        scratch_shapes=[pltpu.VMEM((block, channels), F32), dma((4,))],
        compiler_params=pltpu.CompilerParams(vmem_limit_bytes=4 * 1024 * 1024),
    )(features, grad_one, grad_two, norms)
    return features.reshape(clips, half, channels), grad_one, grad_two, norms


def put_out(features, grad_one, grad_two, norms, features_out, grad_one_out, grad_two_out, norms_out, wide, sem):
    copies = [
        pltpu.make_async_copy(source, target, sem.at[i])
        for i, (source, target) in enumerate(
            (
                (features, features_out),
                (grad_one, grad_one_out),
                (norms, norms_out),
                (wide, grad_two_out),
            )
        )
    ]
    for copy in copies[:3]:
        copy.start()
    wide[...] = grad_two[...].astype(F32)
    copies[3].start()
    for copy in copies:
        copy.wait()


def solution(mesh):
    in_specs = (P("dp", "seq"), P("dp", None), P(), P(), P(), P(), P(), P(), P("dp", "seq", None))
    out_specs = (P("dp", "seq", None), P(), P("seq", None), P())
    return jax.shard_map(
        functools.partial(on_device, mesh.shape["seq"], mesh.shape["dp"] // 2),
        mesh=mesh, in_specs=in_specs, out_specs=out_specs, check_vma=False,
    )
```

```python
import functools

import jax
import jax.numpy as jnp
from jax import lax
from jax.experimental import pallas as pl
from jax.experimental.pallas import tpu as pltpu
from jax.sharding import PartitionSpec as P

MESH = pl.DeviceIdType.MESH
F32, BF16 = jnp.float32, jnp.bfloat16

epsilon = 1e-05
root_half = 0.7071067811865476
normal_peak = 0.3989422804014327

TAPS = 10
STEP = 16
UNROLL = 8
PLAN = ((2, False), (2, False), (2, True))
SEQUENCE = ('m0', 's0', 'f2', 's1', 'm1', 'z0', 'g2', 'z1', 'm2', 'a0', 'a2', 'a1')


def half_erfc_terms():
    scaled = (0.254829592, -0.284496736, 1.421413741, -1.453152027, 1.061405429)
    return [0.5 * term for term in scaled]


def cdf_and_bell(values):
    t = pltpu.reciprocal(1.0 + 0.3275911 * root_half * jnp.abs(values), approx=True)
    bell = jnp.exp(-0.5 * values * values)
    c1, c2, c3, c4, c5 = half_erfc_terms()
    tail = t * (c1 + t * (c2 + t * (c3 + t * (c4 + t * c5)))) * bell
    return jnp.where(values >= 0.0, 1.0 - tail, tail), bell


def slope_of(values, phi):
    return phi + values * jnp.exp(-0.5 * values * values) * normal_peak


def scale_norm(centre):
    inverse = lax.rsqrt(jnp.mean(centre * centre, axis=-1, keepdims=True) + epsilon)
    return centre * inverse, inverse


def layer_norm(pre):
    return scale_norm(pre - jnp.mean(pre, axis=-1, keepdims=True))


def norm_backward(upstream, normed, inverse, gain):
    scaled = upstream * gain
    return inverse * (
        scaled
        - jnp.mean(scaled, axis=-1, keepdims=True)
        - normed * jnp.mean(scaled * normed, axis=-1, keepdims=True)
    )


def fold8(value):
    rows, channels = value.shape
    return jnp.sum(value.reshape(rows // 8, 8, channels), axis=0)


def dot_first(a, b):
    return lax.dot_general(a, b, (((0,), (0,)), ((), ())), preferred_element_type=F32)


def dot_last(a, b):
    return lax.dot_general(a, b, (((1,), (1,)), ((), ())), preferred_element_type=F32)


def kernel(
    ns, nz, parts, early,
    wave_in, lengths_in, conv_one_in, conv_two_in, gain_one_in, shift_one_in, gain_two_in, shift_two_in, cot_in,
    features, grad_one_out, grad_two_out, norms_out,
    wave, lengths, conv_one, conv_two, gain_one, shift_one, gain_two, shift_two, cot, in_s,
    halo, patch, pre, hat, inv, phi, even, patch_two, pre_two, dpre_two, dpre_far, shifted, dact, dhi, dlo,
    order, cot_rows, feat, select,
    mine, from_seq, seq_sum, from_z, from_early, early_sum, from_late, full,
    small, small_core, small_sum, small_seq, small_part, small_z, small_all,
    halo_s, halo_r, p_s, p_r, a_s, a_r, b_s, b_r, c_s, c_r, d_s, d_r, e_s, e_r,
    sa_s, sa_r, sb_s, sb_r, sc_s, sc_r, sd_s, sd_r,
):
    clips, samples = wave.shape
    channels = conv_two.shape[1]
    half = samples // (2 * TAPS // 2)
    rows = clips * half
    middle = channels // 2
    block = mine.shape[1]

    pos = lax.axis_index("seq")
    dp = lax.axis_index("dp")
    z, core = dp // 2, lax.rem(dp, 2)
    partner = dp + 1 - 2 * core

    def at(dp_index, seq_index):
        return {"device_id": (dp_index, seq_index), "device_id_type": MESH}

    def seq_peer(d):
        return lax.rem(pos + d, ns)

    def z_peer(d):
        return lax.rem(z + d, nz)

    loads = [
        pltpu.make_async_copy(source, target, in_s.at[i])
        for i, (source, target) in enumerate(
            (
                (wave_in, wave),
                (conv_one_in, conv_one),
                (gain_one_in, gain_one),
                (shift_one_in, shift_one),
                (lengths_in, lengths),
                (cot_in, cot),
                (gain_two_in, gain_two),
                (shift_two_in, shift_two),
                (conv_two_in, conv_two),
            )
        )
    ]
    for load in loads[:4]:
        load.start()
    barrier = pltpu.get_barrier_semaphore()
    for d in range(1, nz):
        pl.semaphore_signal(barrier, inc=1, **at(2 * z_peer(d) + core, pos))
    for d in range(1, ns):
        pl.semaphore_signal(barrier, inc=1, **at(dp, seq_peer(d)))
    pl.semaphore_signal(barrier, inc=1, **at(partner, pos))
    for load in loads[4:]:
        load.start()

    def iota(shape, dim):
        return lax.broadcasted_iota(jnp.int32, shape, dim)

    for parity in range(2):
        tap = lax.rem(iota((samples, 128), 0) + (TAPS - parity * TAPS // 2), TAPS)
        column = iota((samples, 128), 1)
        select[parity] = jnp.where(
            (tap == lax.rem(column, TAPS)) & (column < 3 * TAPS), 1.0, 0.0
        ).astype(BF16)

    for load in loads[:4]:
        load.wait()
    g1, b1 = gain_one[...], shift_one[...]
    taps = conv_one[...].astype(F32)
    taps = taps - jnp.mean(taps, axis=-1, keepdims=True)
    high = taps.astype(BF16).astype(F32)
    middling = (taps - high).astype(BF16).astype(F32)
    low = taps - high - middling
    thirds = jnp.concatenate([high, middling, low], axis=0).astype(BF16)
    wave_f = wave[...].astype(F32)
    spread = jnp.concatenate([wave_f] * (rows // clips), axis=0)
    lane = iota((rows, samples), 1) - TAPS * (iota((rows, samples), 0) // clips)
    for parity in range(2):
        offset = parity * TAPS // 2
        hit = (lane >= offset) & (lane < offset + TAPS)
        picked = jnp.where(hit, spread, 0.0).astype(BF16)
        found = jnp.dot(picked, select[parity], preferred_element_type=F32)
        patch[parity * rows : (parity + 1) * rows] = found
        pre[parity * rows : (parity + 1) * rows] = jnp.dot(
            found.astype(BF16)[:, 0 : 3 * TAPS], thirds, preferred_element_type=F32
        )

    pl.semaphore_wait(barrier, ns + nz - 1)
    halo_copy = pltpu.make_async_remote_copy(
        wave.at[:, pl.ds(0, 128)], halo, halo_s, halo_r, **at(dp, lax.rem(pos + ns - 1, ns))
    )
    halo_copy.start()

    def forward_one(value):
        normed, inverse = scale_norm(value)
        out = normed * g1 + b1
        probability, _ = cdf_and_bell(out)
        return normed, inverse, probability, out * probability

    def first_rows(r):
        normed, inverse, probability, act = forward_one(pre[pl.ds(r, STEP)])
        hat[pl.ds(r, STEP)] = normed
        inv[pl.ds(r, STEP)] = jnp.broadcast_to(inverse, (STEP, 128))
        phi[pl.ds(r, STEP)] = probability
        return act

    def even_rows(i):
        r = pl.multiple_of(i * STEP, STEP)
        act = first_rows(r)
        even[pl.ds(r, STEP)] = act
        patch_two[pl.ds(r, STEP), pl.ds(0, channels)] = act.astype(BF16)

    def odd_rows(i):
        r = pl.multiple_of(i * STEP, STEP)
        act = first_rows(pl.multiple_of(rows + r, STEP))
        patch_two[pl.ds(r, STEP), pl.ds(channels, channels)] = act.astype(BF16)

    blocks = rows // STEP
    pl.loop(0, blocks, unroll=UNROLL)(even_rows)
    pl.loop(0, blocks - 1, unroll=UNROLL)(odd_rows)

    inside = jnp.where(pos < ns - 1, 1.0, 0.0).astype(F32)
    halo_copy.wait_recv()
    edge = (halo[...].astype(F32) * inside).astype(BF16)
    moved = iota((128, 128), 0) + TAPS // 2
    tap = iota((128, 128), 1)
    fix = jnp.dot(
        edge,
        jnp.where((moved == lax.rem(tap, TAPS)) & (tap < 3 * TAPS), 1.0, 0.0).astype(BF16),
        preferred_element_type=F32,
    )
    three = iota((128, 128), 0) == lax.rem(tap, TAPS)
    tripled = jnp.dot(
        edge, jnp.where(three & (tap < 3 * TAPS), 1.0, 0.0).astype(BF16), preferred_element_type=F32
    )
    last = 2 * rows - clips
    patch[last : last + clips] = patch[last : last + clips] + fix
    fix_pre = jnp.dot(fix.astype(BF16)[:, 0 : 3 * TAPS], thirds, preferred_element_type=F32)
    edge_pre = jnp.dot(tripled.astype(BF16)[:, 0 : 3 * TAPS], thirds, preferred_element_type=F32)
    pre[last : last + clips] = pre[last : last + clips] + fix_pre
    edge_hat, edge_inv, edge_phi, edge_act = forward_one(edge_pre)
    even[rows : rows + clips] = edge_act * inside
    odd_rows(blocks - 1)
    patch_two[0:rows, 2 * channels : 3 * channels] = even[clips : clips + rows].astype(BF16)
    patch_copy = pltpu.make_async_remote_copy(
        patch_two.at[pl.ds(0, rows)], patch_two.at[pl.ds(rows, rows)], p_s, p_r, **at(partner, pos)
    )

    def dpre_copy(which):
        part = pl.ds(which * (rows // 2), rows // 2)
        return pltpu.make_async_remote_copy(
            dpre_two.at[1 - core, part], dpre_far.at[part], a_s.at[which], a_r.at[which], **at(partner, pos)
        )

    patch_copy.start()

    for load in loads[4:6]:
        load.wait()
    clip_of = lax.rem(iota((rows, rows), 0), clips)
    frame_of = iota((rows, rows), 0) // clips
    limit = jnp.full((rows, rows), lengths[0, 0] // TAPS - 1, jnp.int32)
    for c in range(1, clips):
        limit = jnp.where(clip_of == c, lengths[0, c] // TAPS - 1, limit)
    order[...] = jnp.where(
        (iota((rows, rows), 1) == clip_of * half + frame_of) & (pos * half + frame_of < limit), 1.0, 0.0
    ).astype(BF16)
    cot_rows[...] = jnp.dot(order[...], cot[...], preferred_element_type=F32)

    for load in loads[6:]:
        load.wait()
    g2, b2 = gain_two[...], shift_two[...]
    pre_two[...] = jnp.dot(patch_two[0:rows], conv_two[...], preferred_element_type=F32)

    zeros8 = jnp.zeros((8, channels), F32)

    def second(i, sums):
        r = pl.multiple_of(i * STEP, STEP)
        normed, inverse = layer_norm(pre_two[pl.ds(r, STEP)])
        out = normed * g2 + b2
        probability, bell = cdf_and_bell(out)
        feat[pl.ds(r, STEP)] = (out * probability).astype(BF16)
        up = cot_rows[pl.ds(r, STEP)] * (probability + out * bell * normal_peak)
        down = norm_backward(up, normed, inverse, g2).astype(BF16)
        dpre_two[0, pl.ds(r, STEP)] = down[:, 0:middle]
        dpre_two[1, pl.ds(r, STEP)] = down[:, middle:channels]
        return sums[0] + fold8(up * normed), sums[1] + fold8(up)

    sums_two = lax.fori_loop(0, blocks // 2, second, (zeros8, zeros8), unroll=UNROLL)
    dpre_copy(0).start()
    two_hat, two_up = lax.fori_loop(blocks // 2, blocks, second, sums_two, unroll=UNROLL)
    dpre_copy(1).start()

    def back_dot(first):
        return dot_last(dpre_two[0], conv_two[first : first + channels, 0:middle]) + dot_last(
            dpre_two[1], conv_two[first : first + channels, middle:channels]
        )

    shifted[0:8] = jnp.zeros((8, channels), F32)
    shifted[8 : 8 + rows] = back_dot(2 * channels)
    dact[0:rows] = back_dot(0) + shifted[8 - clips : 8 - clips + rows]
    dact[rows : 2 * rows] = back_dot(channels)

    def seq_copy(q, d):
        start, count = parts[q]
        b = seq_peer(d)
        return pltpu.make_async_remote_copy(
            mine.at[b, pl.ds(start, count)], from_seq.at[d - 1, pl.ds(start, count)],
            b_s.at[q, d - 1], b_r.at[q, d - 1], **at(dp, b),
        )

    def pieces_of(q):
        return min(nz, parts[q][1] // 16)

    def z_rows(q, owner):
        piece = parts[q][1] // pieces_of(q)
        return pl.ds(pl.multiple_of(parts[q][0] + owner * piece, 16), piece)

    def z_copy(q, d):
        piece = parts[q][1] // pieces_of(q)
        return pltpu.make_async_remote_copy(
            seq_sum.at[z_rows(q, z_peer(d))], from_z.at[q, d - 1, pl.ds(0, piece)],
            c_s.at[q, d - 1], c_r.at[q, d - 1], **at(2 * z_peer(d) + core, pos),
        )

    def spread_copy(q, d):
        there = full.at[core, z_rows(q, z)]
        return pltpu.make_async_remote_copy(
            there, there, d_s.at[q, d - 1], d_r.at[q, d - 1], **at(2 * z_peer(d) + core, pos)
        )

    def spread_copy_from(q, d):
        there = full.at[core, z_rows(q, z_peer(nz - d))]
        return pltpu.make_async_remote_copy(
            there, there, d_s.at[q, d - 1], d_r.at[q, d - 1], **at(2 * z_peer(d) + core, pos)
        )

    def part_rows(q):
        return pl.ds(parts[q][0], parts[q][1])

    def early_copy(q, d):
        return pltpu.make_async_remote_copy(
            mine.at[:, z_rows(q, z_peer(d))], from_early.at[d - 1],
            c_s.at[q, d - 1], c_r.at[q, d - 1], **at(2 * z_peer(d) + core, pos),
        )

    def late_copy(q, d):
        return pltpu.make_async_remote_copy(
            early_sum.at[seq_peer(d)], from_late.at[d - 1],
            b_s.at[q, d - 1], b_r.at[q, d - 1], **at(dp, seq_peer(d)),
        )

    def relay_copy(q, which):
        there = full.at[which, part_rows(q)]
        return pltpu.make_async_remote_copy(there, there, e_s.at[q], e_r.at[q], **at(partner, pos))

    def when_owner(q, owner, action):
        if pieces_of(q) == nz:
            action()
        else:
            pl.when(owner < pieces_of(q))(action)

    near = dpre_two[core]
    patch_copy.wait_recv()
    for which in range(2):
        dpre_copy(which).wait_recv()
    down = jnp.concatenate([near, dpre_far[...]], axis=0)
    def start_early(q):
        for d in range(1, nz):
            when_owner(q, z_peer(d), lambda d=d: early_copy(q, d).start())

    if block % 128 == 0:
        own = []
        for q in sorted(range(len(parts)), key=lambda q: q not in early):
            start, size = parts[q]
            for d in range(1, ns + 1):
                b = seq_peer(d)
                for first in range(start, start + size, 128):
                    columns = pl.ds(pl.multiple_of(b * block + first, 128), 128)

                    def multiply(b=b, first=first, columns=columns):
                        mine[b, first : first + 128] = dot_first(patch_two[:, columns], down).astype(BF16)

                    if d == ns and q not in early:
                        own.append(multiply)
                    else:
                        multiply()
                if d < ns and q not in early:
                    seq_copy(q, d).start()
            if q in early:
                start_early(q)
        for multiply in own:
            multiply()
    else:
        group = 384
        for i in range(3 * channels // group):
            product = dot_first(patch_two[:, i * group : (i + 1) * group], down).astype(BF16)
            for j in range(group // block):
                mine[i * (group // block) + j] = product[j * block : (j + 1) * block]
        for q in range(len(parts)):
            if q in early:
                start_early(q)
            else:
                for d in range(1, ns):
                    seq_copy(q, d).start()

    def backward_one(incoming, normed, inverse, probability):
        up = incoming * slope_of(normed * g1 + b1, probability)
        return up, norm_backward(up, normed, inverse, g1)

    def back(i, sums):
        at_rows = pl.ds(pl.multiple_of(i * STEP, STEP), STEP)
        normed = hat[at_rows]
        up, dpre = backward_one(dact[at_rows], normed, inv[at_rows, 0:1], phi[at_rows])
        high = dpre.astype(BF16)
        dhi[at_rows] = high
        dlo[at_rows] = (dpre - high.astype(F32)).astype(BF16)
        return sums[0] + fold8(up * normed), sums[1] + fold8(up)

    one_hat, one_up = lax.fori_loop(0, 2 * rows // STEP, back, (zeros8, zeros8), unroll=UNROLL)

    edge_in = shifted[8 + rows - clips : 8 + rows] * inside
    edge_up, edge_dpre = backward_one(edge_in, edge_hat, edge_inv, edge_phi)
    edge_high = edge_dpre.astype(BF16)
    edge_low = (edge_dpre - edge_high.astype(F32)).astype(BF16)

    frames = patch[...].astype(BF16)
    grad_one = (
        dot_first(frames, dhi[...])
        + dot_first(frames, dlo[...])
    )[0:16] + (dot_first(edge, edge_high) + dot_first(edge, edge_low))[0:16]

    def total_row(value):
        return jnp.sum(value, axis=0, keepdims=True)

    sums = (
        (0, grad_one),
        (10, total_row(one_hat) + total_row(edge_up * edge_hat)),
        (11, total_row(one_up) + total_row(edge_up)),
        (12, total_row(two_hat)),
        (13, total_row(two_up)),
        (14, jnp.zeros((2, channels), F32)),
    )
    for row, value in sums:
        for h in range(2):
            small[h, row : row + value.shape[0]] = value[:, h * middle : (h + 1) * middle]

    small_core_copy = pltpu.make_async_remote_copy(
        small.at[1 - core], small_core, sa_s, sa_r, **at(partner, pos)
    )
    small_core_copy.start()

    def small_seq_copy(d):
        return pltpu.make_async_remote_copy(
            small_sum, small_seq.at[pos], sb_s.at[d - 1], sb_r.at[d - 1], **at(dp, seq_peer(d))
        )

    def small_z_copy(d):
        return pltpu.make_async_remote_copy(
            small_part, small_z.at[z], sc_s.at[d - 1], sc_r.at[d - 1], **at(2 * z_peer(d) + core, pos)
        )

    def small_done_copy(which):
        return pltpu.make_async_remote_copy(
            small_all.at[which], small_all.at[which], sd_s, sd_r, **at(partner, pos)
        )

    def seq_done(q):
        span = pl.ds(parts[q][0], parts[q][1])
        total = mine[pos, span].astype(F32)
        for d in range(1, ns):
            seq_copy(q, d).wait_recv()
            total = total + from_seq[d - 1, span].astype(F32)
        value = total.astype(BF16)
        seq_sum[span] = value
        for d in range(1, nz):
            when_owner(q, z_peer(d), lambda d=d: z_copy(q, d).start())

    def z_done(q):
        def action():
            piece = parts[q][1] // pieces_of(q)
            total = seq_sum[z_rows(q, z)].astype(F32)
            for d in range(1, nz):
                z_copy(q, d).wait_recv()
                total = total + from_z[q, d - 1, pl.ds(0, piece)].astype(F32)
            full[core, z_rows(q, z)] = total.astype(BF16)
            for d in range(1, nz):
                spread_copy(q, d).start()

        when_owner(q, z, action)

    def early_done(q):
        def action():
            for d in range(1, nz):
                early_copy(q, d).wait_recv()
            for d in [*range(1, ns), 0]:
                b = seq_peer(d)
                total = mine[b, z_rows(q, z)].astype(F32)
                for other in range(nz - 1):
                    total = total + from_early[other, b].astype(F32)
                early_sum[b] = total.astype(BF16)
                if d:
                    late_copy(q, d).start()

        when_owner(q, z, action)

    def late_done(q):
        def action():
            total = early_sum[pos].astype(F32)
            for d in range(1, ns):
                late_copy(q, d).wait_recv()
                total = total + from_late[d - 1].astype(F32)
            full[core, z_rows(q, z)] = total.astype(BF16)
            for d in range(1, nz):
                spread_copy(q, d).start()

        when_owner(q, z, action)

    def relay(q):
        for d in range(1, nz):
            when_owner(q, z_peer(nz - d), lambda d=d: spread_copy_from(q, d).wait_recv())
        relay_copy(q, core).start()

    features[...] = dot_first(order[...], feat[...]).astype(BF16)

    def small_step(step):
        if step == 0:
            small_core_copy.wait_recv()
            value = (small[core] + small_core[...]).astype(BF16)
            small_part[...] = value
            small_z[z] = value
            for d in range(1, nz):
                small_z_copy(d).start()
        elif step == 1:
            for d in range(1, nz):
                small_z_copy(d).wait_recv()
            total = small_z[0].astype(F32)
            for p in range(1, nz):
                total = total + small_z[p].astype(F32)
            value = total.astype(BF16)
            small_sum[...] = value
            small_seq[pos] = value
            for d in range(1, ns):
                small_seq_copy(d).start()
        else:
            for d in range(1, ns):
                small_seq_copy(d).wait_recv()
            total = small_seq[0].astype(F32)
            for p in range(1, ns):
                total = total + small_seq[p].astype(F32)
            small_all[core] = total
            small_done_copy(core).start()

    events = {"s": seq_done, "z": z_done, "f": early_done, "g": late_done, "a": relay, "m": small_step}
    for event in SEQUENCE:
        events[event[0]](int(event[1]))

    small_done_copy(core).wait_send()
    small_done_copy(1 - core).wait_recv()
    for h in range(2):
        grad_one_out[:, h * middle : (h + 1) * middle] = small_all[h, 0:TAPS]
        norms_out[:, h * middle : (h + 1) * middle] = small_all[h, 10:14]

    small_core_copy.wait_send()
    for d in range(1, nz):
        small_z_copy(d).wait_send()
    for d in range(1, ns):
        small_seq_copy(d).wait_send()
    halo_copy.wait_send()
    patch_copy.wait_send()
    for which in range(2):
        dpre_copy(which).wait_send()
    for q in range(len(parts)):
        if q in early:
            for d in range(1, nz):
                when_owner(q, z_peer(d), lambda q=q, d=d: early_copy(q, d).wait_send())
        else:
            for d in range(1, ns):
                seq_copy(q, d).wait_send()
            for d in range(1, nz):
                when_owner(q, z_peer(d), lambda q=q, d=d: z_copy(q, d).wait_send())

        def sent(q=q):
            if q in early:
                for d in range(1, ns):
                    late_copy(q, d).wait_send()
            for d in range(1, nz):
                spread_copy(q, d).wait_send()

        when_owner(q, z, sent)
        relay_copy(q, core).wait_send()
        relay_copy(q, 1 - core).wait_recv()
    for h in range(2):
        grad_two_out[:, h * middle : (h + 1) * middle] = full[h]


def on_device(ns, nz, waveform, lengths, conv_one, conv_two, gain_one, shift_one, gain_two, shift_two, cotangent):
    clips, samples = waveform.shape
    channels = conv_two.shape[1]
    half = cotangent.shape[1]
    rows = clips * half
    block = conv_two.shape[0] // ns
    unit = block // 6
    parts = tuple(
        (sum(size for size, _ in PLAN[:q]) * unit, size * unit) for q, (size, _) in enumerate(PLAN)
    )
    early = tuple(q for q, (_, over_z) in enumerate(PLAN) if over_z)
    count = len(parts)
    piece = max(size // min(nz, size // 16) for _, size in parts)
    early_piece = max(parts[q][1] // min(nz, parts[q][1] // 16) for q in early)
    middle = channels // 2
    dma = pltpu.SemaphoreType.DMA
    vmem = pl.BlockSpec(memory_space=pltpu.VMEM)
    hbm = pl.BlockSpec(memory_space=pltpu.HBM)
    features, grad_one, grad_two, norms = pl.pallas_call(
        functools.partial(kernel, ns, nz, parts, early),
        out_shape=(
            jax.ShapeDtypeStruct((rows, channels), BF16),
            jax.ShapeDtypeStruct((TAPS, channels), F32),
            jax.ShapeDtypeStruct((block, channels), BF16),
            jax.ShapeDtypeStruct((4, channels), F32),
        ),
        in_specs=[hbm] * 9,
        out_specs=(vmem,) * 4,
        scratch_shapes=[
            pltpu.VMEM(waveform.shape, BF16),
            pltpu.SMEM(lengths.shape, jnp.int32),
            pltpu.VMEM(conv_one.shape, BF16),
            pltpu.VMEM(conv_two.shape, BF16),
            pltpu.VMEM((1, channels), F32),
            pltpu.VMEM((1, channels), F32),
            pltpu.VMEM((1, channels), F32),
            pltpu.VMEM((1, channels), F32),
            pltpu.VMEM((rows, channels), BF16),
            dma((9,)),
            pltpu.VMEM((clips, 128), BF16),
            pltpu.VMEM((2 * rows, 128), F32),
            pltpu.VMEM((2 * rows, channels), F32),
            pltpu.VMEM((2 * rows, channels), F32),
            pltpu.VMEM((2 * rows, 128), F32),
            pltpu.VMEM((2 * rows, channels), F32),
            pltpu.VMEM((rows + 8, channels), F32),
            pltpu.VMEM((2 * rows, 3 * channels), BF16),
            pltpu.VMEM((rows, channels), F32),
            pltpu.VMEM((2, rows, middle), BF16),
            pltpu.VMEM((rows, middle), BF16),
            pltpu.VMEM((rows + 8, channels), F32),
            pltpu.VMEM((2 * rows, channels), F32),
            pltpu.VMEM((2 * rows, channels), BF16),
            pltpu.VMEM((2 * rows, channels), BF16),
            pltpu.VMEM((rows, rows), BF16),
            pltpu.VMEM((rows, channels), F32),
            pltpu.VMEM((rows, channels), BF16),
            pltpu.VMEM((2, samples, 128), BF16),
            pltpu.VMEM((ns, block, middle), BF16),
            pltpu.VMEM((ns - 1, block, middle), BF16),
            pltpu.VMEM((block, middle), BF16),
            pltpu.VMEM((count, nz - 1, piece, middle), BF16),
            pltpu.VMEM((nz - 1, ns, early_piece, middle), BF16),
            pltpu.VMEM((ns, early_piece, middle), BF16),
            pltpu.VMEM((ns - 1, early_piece, middle), BF16),
            pltpu.VMEM((2, block, middle), BF16),
            pltpu.VMEM((2, 16, middle), F32),
            pltpu.VMEM((16, middle), F32),
            pltpu.VMEM((16, middle), BF16),
            pltpu.VMEM((ns, 16, middle), BF16),
            pltpu.VMEM((16, middle), BF16),
            pltpu.VMEM((nz, 16, middle), BF16),
            pltpu.VMEM((2, 16, middle), F32),
            dma, dma,
            dma, dma,
            dma((2,)), dma((2,)),
            dma((count, ns - 1)), dma((count, ns - 1)),
            dma((count, nz - 1)), dma((count, nz - 1)),
            dma((count, nz - 1)), dma((count, nz - 1)),
            dma((count,)), dma((count,)),
            dma, dma,
            dma((ns - 1,)), dma((ns - 1,)),
            dma((nz - 1,)), dma((nz - 1,)),
            dma, dma,
        ],
        compiler_params=pltpu.CompilerParams(
            collective_id=0, has_side_effects=True, vmem_limit_bytes=48 * 1024 * 1024
        ),
    )(
        *[
            pltpu.with_memory_space_constraint(value, pltpu.HBM)
            for value in (
        waveform,
        lengths,
        conv_one,
        conv_two,
        gain_one.reshape(1, channels),
        shift_one.reshape(1, channels),
        gain_two.reshape(1, channels),
        shift_two.reshape(1, channels),
        cotangent.reshape(rows, channels),
    )])
    features, grad_one, grad_two, norms = pl.pallas_call(
        put_out,
        out_shape=(
            jax.ShapeDtypeStruct((rows, channels), BF16),
            jax.ShapeDtypeStruct((TAPS, channels), F32),
            jax.ShapeDtypeStruct((block, channels), F32),
            jax.ShapeDtypeStruct((4, channels), F32),
        ),
        in_specs=[vmem] * 4,
        out_specs=(hbm,) * 4,
        scratch_shapes=[pltpu.VMEM((block, channels), F32), dma((4,))],
        compiler_params=pltpu.CompilerParams(vmem_limit_bytes=4 * 1024 * 1024),
    )(features, grad_one, grad_two, norms)
    return features.reshape(clips, half, channels), grad_one, grad_two, norms


def put_out(features, grad_one, grad_two, norms, features_out, grad_one_out, grad_two_out, norms_out, wide, sem):
    copies = [
        pltpu.make_async_copy(source, target, sem.at[i])
        for i, (source, target) in enumerate(
            (
                (features, features_out),
                (grad_one, grad_one_out),
                (norms, norms_out),
                (wide, grad_two_out),
            )
        )
    ]
    for copy in copies[:3]:
        copy.start()
    wide[...] = grad_two[...].astype(F32)
    copies[3].start()
    for copy in copies:
        copy.wait()


def solution(mesh):
    in_specs = (P("dp", "seq"), P("dp", None), P(), P(), P(), P(), P(), P(), P("dp", "seq", None))
    out_specs = (P("dp", "seq", None), P(), P("seq", None), P())
    return jax.shard_map(
        functools.partial(on_device, mesh.shape["seq"], mesh.shape["dp"] // 2),
        mesh=mesh, in_specs=in_specs, out_specs=out_specs, check_vma=False,
    )
```

```python
import functools

import jax
import jax.numpy as jnp
from jax import lax
from jax.experimental import pallas as pl
from jax.experimental.pallas import tpu as pltpu
from jax.sharding import PartitionSpec as P

MESH = pl.DeviceIdType.MESH
F32, BF16 = jnp.float32, jnp.bfloat16

epsilon = 1e-05
root_half = 0.7071067811865476
normal_peak = 0.3989422804014327

TAPS = 10
TENTH = 6554
STEP = 16
UNROLL = 8
PLAN = ((2, False), (2, False), (2, True))
SEQUENCE = ('m0', 's0', 'f2', 's1', 'm1', 'z0', 'g2', 'z1', 'm2', 'a0', 'a2', 'a1')


def half_erfc_terms():
    scaled = (0.254829592, -0.284496736, 1.421413741, -1.453152027, 1.061405429)
    return [0.5 * term for term in scaled]


def cdf_and_bell(values):
    t = pltpu.reciprocal(1.0 + 0.3275911 * root_half * jnp.abs(values), approx=True)
    bell = jnp.exp(-0.5 * values * values)
    c1, c2, c3, c4, c5 = half_erfc_terms()
    tail = t * (c1 + t * (c2 + t * (c3 + t * (c4 + t * c5)))) * bell
    return jnp.where(values >= 0.0, 1.0 - tail, tail), bell


def slope_of(values, phi):
    return phi + values * jnp.exp(-0.5 * values * values) * normal_peak


def scale_norm(centre):
    inverse = lax.rsqrt(jnp.mean(centre * centre, axis=-1, keepdims=True) + epsilon)
    return centre * inverse, inverse


def layer_norm(pre):
    return scale_norm(pre - jnp.mean(pre, axis=-1, keepdims=True))


def norm_backward(upstream, normed, inverse, gain):
    scaled = upstream * gain
    return inverse * (
        scaled
        - jnp.mean(scaled, axis=-1, keepdims=True)
        - normed * jnp.mean(scaled * normed, axis=-1, keepdims=True)
    )


def fold8(value):
    rows, channels = value.shape
    return jnp.sum(value.reshape(rows // 8, 8, channels), axis=0)


def dot_first(a, b):
    return lax.dot_general(a, b, (((0,), (0,)), ((), ())), preferred_element_type=F32)


def dot_last(a, b):
    return lax.dot_general(a, b, (((1,), (1,)), ((), ())), preferred_element_type=F32)


def kernel(
    ns, nz, parts, early,
    wave_in, lengths_in, conv_one_in, conv_two_in, gain_one_in, shift_one_in, gain_two_in, shift_two_in, cot_in,
    features, grad_one_out, grad_two_out, norms_out,
    wave, lengths, conv_one, conv_two, gain_one, shift_one, gain_two, shift_two, cot, in_s,
    halo, patch, pre, hat, inv, phi, even, patch_two, pre_two, dpre_two, dpre_far, shifted, dact, dhi, dlo,
    order, cot_rows, feat, select,
    mine, from_seq, seq_sum, from_z, from_early, early_sum, from_late, full,
    small, small_core, small_sum, small_seq, small_part, small_z, small_all,
    halo_s, halo_r, p_s, p_r, a_s, a_r, b_s, b_r, c_s, c_r, d_s, d_r, e_s, e_r,
    sa_s, sa_r, sb_s, sb_r, sc_s, sc_r, sd_s, sd_r,
):
    clips, samples = wave.shape
    channels = conv_two.shape[1]
    half = samples // (2 * TAPS // 2)
    rows = clips * half
    middle = channels // 2
    block = mine.shape[1]

    pos = lax.axis_index("seq")
    dp = lax.axis_index("dp")
    z, core = dp // 2, lax.rem(dp, 2)
    partner = dp + 1 - 2 * core

    def at(dp_index, seq_index):
        return {"device_id": (dp_index, seq_index), "device_id_type": MESH}

    def seq_peer(d):
        return lax.rem(pos + d, ns)

    def z_peer(d):
        return lax.rem(z + d, nz)

    loads = [
        pltpu.make_async_copy(source, target, in_s.at[i])
        for i, (source, target) in enumerate(
            (
                (wave_in, wave),
                (conv_one_in, conv_one),
                (gain_one_in, gain_one),
                (shift_one_in, shift_one),
                (lengths_in, lengths),
                (cot_in, cot),
                (gain_two_in, gain_two),
                (shift_two_in, shift_two),
                (conv_two_in, conv_two),
            )
        )
    ]
    for load in loads[:4]:
        load.start()
    barrier = pltpu.get_barrier_semaphore()
    for d in range(1, nz):
        pl.semaphore_signal(barrier, inc=1, **at(2 * z_peer(d) + core, pos))
    for d in range(1, ns):
        pl.semaphore_signal(barrier, inc=1, **at(dp, seq_peer(d)))
    pl.semaphore_signal(barrier, inc=1, **at(partner, pos))
    for load in loads[4:]:
        load.start()

    def iota(shape, dim):
        return lax.broadcasted_iota(jnp.int32, shape, dim)

    sample = iota((samples, 128), 0)
    tap_of = sample - TAPS * lax.shift_right_logical(sample * TENTH, 16)
    column = iota((8, 128), 1)
    for parity in range(2):
        wanted = lax.rem(column + parity * TAPS // 2, TAPS)
        wanted = jnp.where(column < 3 * TAPS, wanted, -1)[0:1]
        select[parity] = jnp.where(tap_of == wanted, 1.0, 0.0).astype(BF16)

    for load in loads[:4]:
        load.wait()
    g1, b1 = gain_one[...], shift_one[...]
    taps = conv_one[...].astype(F32)
    taps = taps - jnp.mean(taps, axis=-1, keepdims=True)
    high = taps.astype(BF16).astype(F32)
    middling = (taps - high).astype(BF16).astype(F32)
    low = taps - high - middling
    thirds = jnp.concatenate([high, middling, low], axis=0).astype(BF16)
    wave_f = wave[...].astype(F32)
    spread = jnp.concatenate([wave_f] * (rows // clips), axis=0)
    lane = iota((rows, samples), 1) - TAPS * lax.div(iota((rows, samples), 0), clips)
    for parity in range(2):
        offset = parity * TAPS // 2
        hit = (lane >= offset) & (lane < offset + TAPS)
        picked = jnp.where(hit, spread, 0.0).astype(BF16)
        found = jnp.dot(picked, select[parity], preferred_element_type=F32)
        patch[parity * rows : (parity + 1) * rows] = found
        pre[parity * rows : (parity + 1) * rows] = jnp.dot(
            found.astype(BF16)[:, 0 : 3 * TAPS], thirds, preferred_element_type=F32
        )

    def forward_one(value):
        normed, inverse = scale_norm(value)
        out = normed * g1 + b1
        probability, _ = cdf_and_bell(out)
        return normed, inverse, probability, out * probability

    def first_rows(r):
        normed, inverse, probability, act = forward_one(pre[pl.ds(r, STEP)])
        hat[pl.ds(r, STEP)] = normed
        inv[pl.ds(r, STEP)] = jnp.broadcast_to(inverse, (STEP, 128))
        phi[pl.ds(r, STEP)] = probability
        return act

    def even_rows(i):
        r = pl.multiple_of(i * STEP, STEP)
        act = first_rows(r)
        even[pl.ds(r, STEP)] = act
        patch_two[pl.ds(r, STEP), pl.ds(0, channels)] = act.astype(BF16)

    def odd_rows(i):
        r = pl.multiple_of(i * STEP, STEP)
        act = first_rows(pl.multiple_of(rows + r, STEP))
        patch_two[pl.ds(r, STEP), pl.ds(channels, channels)] = act.astype(BF16)

    blocks = rows // STEP
    pl.loop(0, blocks, unroll=UNROLL)(even_rows)
    pl.semaphore_wait(barrier, ns + nz - 1)
    halo_copy = pltpu.make_async_remote_copy(
        wave.at[:, pl.ds(0, 128)], halo, halo_s, halo_r, **at(dp, lax.rem(pos + ns - 1, ns))
    )
    halo_copy.start()

    pl.loop(0, blocks - 1, unroll=UNROLL)(odd_rows)

    for load in loads[4:6]:
        load.wait()
    clip_of = lax.rem(iota((rows, rows), 0), clips)
    frame_of = lax.div(iota((rows, rows), 0), clips)
    limit = jnp.full((rows, rows), lengths[0, 0] // TAPS - 1, jnp.int32)
    for c in range(1, clips):
        limit = jnp.where(clip_of == c, lengths[0, c] // TAPS - 1, limit)
    order[...] = jnp.where(
        (iota((rows, rows), 1) == clip_of * half + frame_of) & (pos * half + frame_of < limit), 1.0, 0.0
    ).astype(BF16)
    cot_rows[...] = jnp.dot(order[...], cot[...], preferred_element_type=F32)

    inside = jnp.where(pos < ns - 1, 1.0, 0.0).astype(F32)
    last = 2 * rows - clips
    late = jnp.concatenate([taps[TAPS // 2 : TAPS], jnp.zeros((TAPS // 2, channels), F32)], axis=0)
    both = jnp.concatenate([taps, late], axis=1)
    both_high = both.astype(BF16)
    both_rest = both - both_high.astype(F32)
    both_middle = both_rest.astype(BF16)
    both_low = (both_rest - both_middle.astype(F32)).astype(BF16)
    halo_copy.wait_recv()
    edge = (halo[...].astype(F32) * inside).astype(BF16)
    edges = sum(
        jnp.dot(edge[:, 0:TAPS], part, preferred_element_type=F32)
        for part in (both_low, both_middle, both_high)
    )
    pre[last : last + clips] = pre[last : last + clips] + edges[:, channels : 2 * channels]
    edge_hat, edge_inv, edge_phi, edge_act = forward_one(edges[:, 0:channels])
    even[rows : rows + clips] = edge_act * inside
    odd_rows(blocks - 1)
    patch_two[0:rows, 2 * channels : 3 * channels] = even[clips : clips + rows].astype(BF16)
    patch_copy = pltpu.make_async_remote_copy(
        patch_two.at[pl.ds(0, rows)], patch_two.at[pl.ds(rows, rows)], p_s, p_r, **at(partner, pos)
    )

    def dpre_copy(which):
        part = pl.ds(which * (rows // 2), rows // 2)
        return pltpu.make_async_remote_copy(
            dpre_two.at[1 - core, part], dpre_far.at[part], a_s.at[which], a_r.at[which], **at(partner, pos)
        )

    patch_copy.start()

    for load in loads[6:]:
        load.wait()
    g2, b2 = gain_two[...], shift_two[...]
    pre_two[...] = jnp.dot(patch_two[0:rows], conv_two[...], preferred_element_type=F32)

    zeros8 = jnp.zeros((8, channels), F32)

    def second(i, sums):
        r = pl.multiple_of(i * STEP, STEP)
        normed, inverse = layer_norm(pre_two[pl.ds(r, STEP)])
        out = normed * g2 + b2
        probability, bell = cdf_and_bell(out)
        feat[pl.ds(r, STEP)] = (out * probability).astype(BF16)
        up = cot_rows[pl.ds(r, STEP)] * (probability + out * bell * normal_peak)
        down = norm_backward(up, normed, inverse, g2).astype(BF16)
        dpre_two[0, pl.ds(r, STEP)] = down[:, 0:middle]
        dpre_two[1, pl.ds(r, STEP)] = down[:, middle:channels]
        return sums[0] + fold8(up * normed), sums[1] + fold8(up)

    sums_two = lax.fori_loop(0, blocks // 2, second, (zeros8, zeros8), unroll=UNROLL)
    dpre_copy(0).start()
    two_hat, two_up = lax.fori_loop(blocks // 2, blocks, second, sums_two, unroll=UNROLL)
    dpre_copy(1).start()

    def back_dot(first):
        return dot_last(dpre_two[0], conv_two[first : first + channels, 0:middle]) + dot_last(
            dpre_two[1], conv_two[first : first + channels, middle:channels]
        )

    shifted[0:8] = jnp.zeros((8, channels), F32)
    shifted[8 : 8 + rows] = back_dot(2 * channels)
    dact[0:rows] = back_dot(0) + shifted[8 - clips : 8 - clips + rows]
    dact[rows : 2 * rows] = back_dot(channels)

    def seq_copy(q, d):
        start, count = parts[q]
        b = seq_peer(d)
        return pltpu.make_async_remote_copy(
            mine.at[b, pl.ds(start, count)], from_seq.at[d - 1, pl.ds(start, count)],
            b_s.at[q, d - 1], b_r.at[q, d - 1], **at(dp, b),
        )

    def pieces_of(q):
        return min(nz, parts[q][1] // 16)

    def z_rows(q, owner):
        piece = parts[q][1] // pieces_of(q)
        return pl.ds(pl.multiple_of(parts[q][0] + owner * piece, 16), piece)

    def z_copy(q, d):
        piece = parts[q][1] // pieces_of(q)
        return pltpu.make_async_remote_copy(
            seq_sum.at[z_rows(q, z_peer(d))], from_z.at[q, d - 1, pl.ds(0, piece)],
            c_s.at[q, d - 1], c_r.at[q, d - 1], **at(2 * z_peer(d) + core, pos),
        )

    def spread_copy(q, d):
        there = full.at[core, z_rows(q, z)]
        return pltpu.make_async_remote_copy(
            there, there, d_s.at[q, d - 1], d_r.at[q, d - 1], **at(2 * z_peer(d) + core, pos)
        )

    def spread_copy_from(q, d):
        there = full.at[core, z_rows(q, z_peer(nz - d))]
        return pltpu.make_async_remote_copy(
            there, there, d_s.at[q, d - 1], d_r.at[q, d - 1], **at(2 * z_peer(d) + core, pos)
        )

    def part_rows(q):
        return pl.ds(parts[q][0], parts[q][1])

    def early_copy(q, d):
        return pltpu.make_async_remote_copy(
            mine.at[:, z_rows(q, z_peer(d))], from_early.at[d - 1],
            c_s.at[q, d - 1], c_r.at[q, d - 1], **at(2 * z_peer(d) + core, pos),
        )

    def late_copy(q, d):
        return pltpu.make_async_remote_copy(
            early_sum.at[seq_peer(d)], from_late.at[d - 1],
            b_s.at[q, d - 1], b_r.at[q, d - 1], **at(dp, seq_peer(d)),
        )

    def relay_copy(q, which):
        there = full.at[which, part_rows(q)]
        return pltpu.make_async_remote_copy(there, there, e_s.at[q], e_r.at[q], **at(partner, pos))

    def when_owner(q, owner, action):
        if pieces_of(q) == nz:
            action()
        else:
            pl.when(owner < pieces_of(q))(action)

    near = dpre_two[core]
    features[...] = dot_first(order[...], feat[...]).astype(BF16)
    patch_copy.wait_recv()
    for which in range(2):
        dpre_copy(which).wait_recv()
    down = jnp.concatenate([near, dpre_far[...]], axis=0)
    def start_early(q):
        for d in range(1, nz):
            when_owner(q, z_peer(d), lambda d=d: early_copy(q, d).start())

    if block % 128 == 0:
        own = []
        for q in sorted(range(len(parts)), key=lambda q: q not in early):
            start, size = parts[q]
            for d in range(1, ns + 1):
                b = seq_peer(d)
                for first in range(start, start + size, 128):
                    columns = pl.ds(pl.multiple_of(b * block + first, 128), 128)

                    def multiply(b=b, first=first, columns=columns):
                        mine[b, first : first + 128] = dot_first(patch_two[:, columns], down).astype(BF16)

                    if d == ns and q not in early:
                        own.append(multiply)
                    else:
                        multiply()
                if d < ns and q not in early:
                    seq_copy(q, d).start()
            if q in early:
                start_early(q)
        for multiply in own:
            multiply()
    else:
        group = 384
        for i in range(3 * channels // group):
            product = dot_first(patch_two[:, i * group : (i + 1) * group], down).astype(BF16)
            for j in range(group // block):
                mine[i * (group // block) + j] = product[j * block : (j + 1) * block]
        for q in range(len(parts)):
            if q in early:
                start_early(q)
            else:
                for d in range(1, ns):
                    seq_copy(q, d).start()

    def backward_one(incoming, normed, inverse, probability):
        up = incoming * slope_of(normed * g1 + b1, probability)
        return up, norm_backward(up, normed, inverse, g1)

    def back(i, sums):
        at_rows = pl.ds(pl.multiple_of(i * STEP, STEP), STEP)
        normed = hat[at_rows]
        up, dpre = backward_one(dact[at_rows], normed, inv[at_rows, 0:1], phi[at_rows])
        high = dpre.astype(BF16)
        dhi[at_rows] = high
        dlo[at_rows] = (dpre - high.astype(F32)).astype(BF16)
        return sums[0] + fold8(up * normed), sums[1] + fold8(up)

    one_hat, one_up = lax.fori_loop(0, 2 * rows // STEP, back, (zeros8, zeros8), unroll=UNROLL)

    edge_in = shifted[8 + rows - clips : 8 + rows] * inside
    edge_up, edge_dpre = backward_one(edge_in, edge_hat, edge_inv, edge_phi)
    edge_high = edge_dpre.astype(BF16)
    edge_low = (edge_dpre - edge_high.astype(F32)).astype(BF16)

    moved = iota((128, 128), 0) + TAPS // 2
    tap = iota((128, 128), 1)
    fix = jnp.dot(
        edge, jnp.where((moved == tap) & (tap < TAPS), 1.0, 0.0).astype(BF16), preferred_element_type=F32
    )
    patch[last : last + clips] = patch[last : last + clips] + fix
    frames = patch[...].astype(BF16)
    grad_one = (
        dot_first(frames, dhi[...])
        + dot_first(frames, dlo[...])
    )[0:16] + (dot_first(edge, edge_high) + dot_first(edge, edge_low))[0:16]

    def total_row(value):
        return jnp.sum(value, axis=0, keepdims=True)

    sums = (
        (0, grad_one),
        (10, total_row(one_hat) + total_row(edge_up * edge_hat)),
        (11, total_row(one_up) + total_row(edge_up)),
        (12, total_row(two_hat)),
        (13, total_row(two_up)),
        (14, jnp.zeros((2, channels), F32)),
    )
    for row, value in sums:
        for h in range(2):
            small[h, row : row + value.shape[0]] = value[:, h * middle : (h + 1) * middle]

    small_core_copy = pltpu.make_async_remote_copy(
        small.at[1 - core], small_core, sa_s, sa_r, **at(partner, pos)
    )
    small_core_copy.start()

    def small_seq_copy(d):
        return pltpu.make_async_remote_copy(
            small_sum, small_seq.at[pos], sb_s.at[d - 1], sb_r.at[d - 1], **at(dp, seq_peer(d))
        )

    def small_z_copy(d):
        return pltpu.make_async_remote_copy(
            small_part, small_z.at[z], sc_s.at[d - 1], sc_r.at[d - 1], **at(2 * z_peer(d) + core, pos)
        )

    def small_done_copy(which):
        return pltpu.make_async_remote_copy(
            small_all.at[which], small_all.at[which], sd_s, sd_r, **at(partner, pos)
        )

    def seq_done(q):
        span = pl.ds(parts[q][0], parts[q][1])
        total = mine[pos, span].astype(F32)
        for d in range(1, ns):
            seq_copy(q, d).wait_recv()
            total = total + from_seq[d - 1, span].astype(F32)
        value = total.astype(BF16)
        seq_sum[span] = value
        for d in range(1, nz):
            when_owner(q, z_peer(d), lambda d=d: z_copy(q, d).start())

    def z_done(q):
        def action():
            piece = parts[q][1] // pieces_of(q)
            total = seq_sum[z_rows(q, z)].astype(F32)
            for d in range(1, nz):
                z_copy(q, d).wait_recv()
                total = total + from_z[q, d - 1, pl.ds(0, piece)].astype(F32)
            full[core, z_rows(q, z)] = total.astype(BF16)
            for d in range(1, nz):
                spread_copy(q, d).start()

        when_owner(q, z, action)

    def early_done(q):
        def action():
            for d in range(1, nz):
                early_copy(q, d).wait_recv()
            for d in [*range(1, ns), 0]:
                b = seq_peer(d)
                total = mine[b, z_rows(q, z)].astype(F32)
                for other in range(nz - 1):
                    total = total + from_early[other, b].astype(F32)
                early_sum[b] = total.astype(BF16)
                if d:
                    late_copy(q, d).start()

        when_owner(q, z, action)

    def late_done(q):
        def action():
            total = early_sum[pos].astype(F32)
            for d in range(1, ns):
                late_copy(q, d).wait_recv()
                total = total + from_late[d - 1].astype(F32)
            full[core, z_rows(q, z)] = total.astype(BF16)
            for d in range(1, nz):
                spread_copy(q, d).start()

        when_owner(q, z, action)

    def relay(q):
        for d in range(1, nz):
            when_owner(q, z_peer(nz - d), lambda d=d: spread_copy_from(q, d).wait_recv())
        relay_copy(q, core).start()

    def small_step(step):
        if step == 0:
            small_core_copy.wait_recv()
            value = (small[core] + small_core[...]).astype(BF16)
            small_part[...] = value
            small_z[z] = value
            for d in range(1, nz):
                small_z_copy(d).start()
        elif step == 1:
            for d in range(1, nz):
                small_z_copy(d).wait_recv()
            total = small_z[0].astype(F32)
            for p in range(1, nz):
                total = total + small_z[p].astype(F32)
            value = total.astype(BF16)
            small_sum[...] = value
            small_seq[pos] = value
            for d in range(1, ns):
                small_seq_copy(d).start()
        else:
            for d in range(1, ns):
                small_seq_copy(d).wait_recv()
            total = small_seq[0].astype(F32)
            for p in range(1, ns):
                total = total + small_seq[p].astype(F32)
            small_all[core] = total
            small_done_copy(core).start()

    events = {"s": seq_done, "z": z_done, "f": early_done, "g": late_done, "a": relay, "m": small_step}
    for event in SEQUENCE:
        events[event[0]](int(event[1]))

    small_done_copy(core).wait_send()
    small_done_copy(1 - core).wait_recv()
    for h in range(2):
        grad_one_out[:, h * middle : (h + 1) * middle] = small_all[h, 0:TAPS]
        norms_out[:, h * middle : (h + 1) * middle] = small_all[h, 10:14]

    small_core_copy.wait_send()
    for d in range(1, nz):
        small_z_copy(d).wait_send()
    for d in range(1, ns):
        small_seq_copy(d).wait_send()
    halo_copy.wait_send()
    patch_copy.wait_send()
    for which in range(2):
        dpre_copy(which).wait_send()
    for q in range(len(parts)):
        if q in early:
            for d in range(1, nz):
                when_owner(q, z_peer(d), lambda q=q, d=d: early_copy(q, d).wait_send())
        else:
            for d in range(1, ns):
                seq_copy(q, d).wait_send()
            for d in range(1, nz):
                when_owner(q, z_peer(d), lambda q=q, d=d: z_copy(q, d).wait_send())

        def sent(q=q):
            if q in early:
                for d in range(1, ns):
                    late_copy(q, d).wait_send()
            for d in range(1, nz):
                spread_copy(q, d).wait_send()

        when_owner(q, z, sent)
    for q in [int(event[1]) for event in SEQUENCE if event[0] == "a"]:
        start, size = parts[q]
        grad_two_out[start : start + size, pl.ds(pl.multiple_of(core * middle, 128), middle)] = full[core, part_rows(q)]
        relay_copy(q, core).wait_send()
        relay_copy(q, 1 - core).wait_recv()
        grad_two_out[start : start + size, pl.ds(pl.multiple_of((1 - core) * middle, 128), middle)] = full[
            1 - core, part_rows(q)
        ]


def on_device(ns, nz, waveform, lengths, conv_one, conv_two, gain_one, shift_one, gain_two, shift_two, cotangent):
    clips, samples = waveform.shape
    channels = conv_two.shape[1]
    half = cotangent.shape[1]
    rows = clips * half
    block = conv_two.shape[0] // ns
    unit = block // 6
    parts = tuple(
        (sum(size for size, _ in PLAN[:q]) * unit, size * unit) for q, (size, _) in enumerate(PLAN)
    )
    early = tuple(q for q, (_, over_z) in enumerate(PLAN) if over_z)
    count = len(parts)
    piece = max(size // min(nz, size // 16) for _, size in parts)
    early_piece = max(parts[q][1] // min(nz, parts[q][1] // 16) for q in early)
    middle = channels // 2
    dma = pltpu.SemaphoreType.DMA
    vmem = pl.BlockSpec(memory_space=pltpu.VMEM)
    hbm = pl.BlockSpec(memory_space=pltpu.HBM)
    features, grad_one, grad_two, norms = pl.pallas_call(
        functools.partial(kernel, ns, nz, parts, early),
        out_shape=(
            jax.ShapeDtypeStruct((rows, channels), BF16),
            jax.ShapeDtypeStruct((TAPS, channels), F32),
            jax.ShapeDtypeStruct((block, channels), BF16),
            jax.ShapeDtypeStruct((4, channels), F32),
        ),
        in_specs=[hbm] * 9,
        out_specs=(vmem,) * 4,
        scratch_shapes=[
            pltpu.VMEM(waveform.shape, BF16),
            pltpu.SMEM(lengths.shape, jnp.int32),
            pltpu.VMEM(conv_one.shape, BF16),
            pltpu.VMEM(conv_two.shape, BF16),
            pltpu.VMEM((1, channels), F32),
            pltpu.VMEM((1, channels), F32),
            pltpu.VMEM((1, channels), F32),
            pltpu.VMEM((1, channels), F32),
            pltpu.VMEM((rows, channels), BF16),
            dma((9,)),
            pltpu.VMEM((clips, 128), BF16),
            pltpu.VMEM((2 * rows, 128), F32),
            pltpu.VMEM((2 * rows, channels), F32),
            pltpu.VMEM((2 * rows, channels), F32),
            pltpu.VMEM((2 * rows, 128), F32),
            pltpu.VMEM((2 * rows, channels), F32),
            pltpu.VMEM((rows + 8, channels), F32),
            pltpu.VMEM((2 * rows, 3 * channels), BF16),
            pltpu.VMEM((rows, channels), F32),
            pltpu.VMEM((2, rows, middle), BF16),
            pltpu.VMEM((rows, middle), BF16),
            pltpu.VMEM((rows + 8, channels), F32),
            pltpu.VMEM((2 * rows, channels), F32),
            pltpu.VMEM((2 * rows, channels), BF16),
            pltpu.VMEM((2 * rows, channels), BF16),
            pltpu.VMEM((rows, rows), BF16),
            pltpu.VMEM((rows, channels), F32),
            pltpu.VMEM((rows, channels), BF16),
            pltpu.VMEM((2, samples, 128), BF16),
            pltpu.VMEM((ns, block, middle), BF16),
            pltpu.VMEM((ns - 1, block, middle), BF16),
            pltpu.VMEM((block, middle), BF16),
            pltpu.VMEM((count, nz - 1, piece, middle), BF16),
            pltpu.VMEM((nz - 1, ns, early_piece, middle), BF16),
            pltpu.VMEM((ns, early_piece, middle), BF16),
            pltpu.VMEM((ns - 1, early_piece, middle), BF16),
            pltpu.VMEM((2, block, middle), BF16),
            pltpu.VMEM((2, 16, middle), F32),
            pltpu.VMEM((16, middle), F32),
            pltpu.VMEM((16, middle), BF16),
            pltpu.VMEM((ns, 16, middle), BF16),
            pltpu.VMEM((16, middle), BF16),
            pltpu.VMEM((nz, 16, middle), BF16),
            pltpu.VMEM((2, 16, middle), F32),
            dma, dma,
            dma, dma,
            dma((2,)), dma((2,)),
            dma((count, ns - 1)), dma((count, ns - 1)),
            dma((count, nz - 1)), dma((count, nz - 1)),
            dma((count, nz - 1)), dma((count, nz - 1)),
            dma((count,)), dma((count,)),
            dma, dma,
            dma((ns - 1,)), dma((ns - 1,)),
            dma((nz - 1,)), dma((nz - 1,)),
            dma, dma,
        ],
        compiler_params=pltpu.CompilerParams(
            collective_id=0, has_side_effects=True, vmem_limit_bytes=48 * 1024 * 1024
        ),
    )(
        *[
            pltpu.with_memory_space_constraint(value, pltpu.HBM)
            for value in (
        waveform,
        lengths,
        conv_one,
        conv_two,
        gain_one.reshape(1, channels),
        shift_one.reshape(1, channels),
        gain_two.reshape(1, channels),
        shift_two.reshape(1, channels),
        cotangent.reshape(rows, channels),
    )])
    features, grad_one, grad_two, norms = pl.pallas_call(
        put_out,
        out_shape=(
            jax.ShapeDtypeStruct((rows, channels), BF16),
            jax.ShapeDtypeStruct((TAPS, channels), F32),
            jax.ShapeDtypeStruct((block, channels), F32),
            jax.ShapeDtypeStruct((4, channels), F32),
        ),
        in_specs=[vmem] * 4,
        out_specs=(hbm,) * 4,
        scratch_shapes=[pltpu.VMEM((block, channels), F32), dma((6,))],
        compiler_params=pltpu.CompilerParams(vmem_limit_bytes=4 * 1024 * 1024),
    )(features, grad_one, grad_two, norms)
    return features.reshape(clips, half, channels), grad_one, grad_two, norms


def put_out(features, grad_one, grad_two, norms, features_out, grad_one_out, grad_two_out, norms_out, wide, sem):
    rows = wide.shape[0] // 3
    copies = [
        pltpu.make_async_copy(source, target, sem.at[i])
        for i, (source, target) in enumerate(
            ((features, features_out), (grad_one, grad_one_out), (norms, norms_out))
        )
    ]
    for copy in copies:
        copy.start()
    for i in range(3):
        part = pl.ds(i * rows, rows)
        wide[part] = grad_two[part].astype(F32)
        copies.append(pltpu.make_async_copy(wide.at[part], grad_two_out.at[part], sem.at[3 + i]))
        copies[-1].start()
    for copy in copies:
        copy.wait()


def solution(mesh):
    in_specs = (P("dp", "seq"), P("dp", None), P(), P(), P(), P(), P(), P(), P("dp", "seq", None))
    out_specs = (P("dp", "seq", None), P(), P("seq", None), P())
    return jax.shard_map(
        functools.partial(on_device, mesh.shape["seq"], mesh.shape["dp"] // 2),
        mesh=mesh, in_specs=in_specs, out_specs=out_specs, check_vma=False,
    )
```

```python
import functools

import jax
import jax.numpy as jnp
from jax import lax
from jax.experimental import pallas as pl
from jax.experimental.pallas import tpu as pltpu
from jax.sharding import PartitionSpec as P

MESH = pl.DeviceIdType.MESH
F32, BF16 = jnp.float32, jnp.bfloat16

epsilon = 1e-05
root_half = 0.7071067811865476
normal_peak = 0.3989422804014327

TAPS = 10
TENTH = 6554
STEP = 16
UNROLL = 8
PLAN = ((2, False), (2, False), (2, True))
CROSSED = 1
SEQUENCE = ('m0', 's0', 'f2', 's1', 'm1', 'z0', 'g2', 'z1', 'm2', 'a0', 'a2', 'a1')


def half_erfc_terms():
    scaled = (0.254829592, -0.284496736, 1.421413741, -1.453152027, 1.061405429)
    return [0.5 * term for term in scaled]


def cdf_and_bell(values):
    t = pltpu.reciprocal(1.0 + 0.3275911 * root_half * jnp.abs(values), approx=True)
    bell = jnp.exp(-0.5 * values * values)
    c1, c2, c3, c4, c5 = half_erfc_terms()
    tail = t * (c1 + t * (c2 + t * (c3 + t * (c4 + t * c5)))) * bell
    return jnp.where(values >= 0.0, 1.0 - tail, tail), bell


def slope_of(values, phi):
    return phi + values * jnp.exp(-0.5 * values * values) * normal_peak


def scale_norm(centre):
    inverse = lax.rsqrt(jnp.mean(centre * centre, axis=-1, keepdims=True) + epsilon)
    return centre * inverse, inverse


def layer_norm(pre):
    return scale_norm(pre - jnp.mean(pre, axis=-1, keepdims=True))


def norm_backward(upstream, normed, inverse, gain):
    scaled = upstream * gain
    return inverse * (
        scaled
        - jnp.mean(scaled, axis=-1, keepdims=True)
        - normed * jnp.mean(scaled * normed, axis=-1, keepdims=True)
    )


def fold8(value):
    rows, channels = value.shape
    return jnp.sum(value.reshape(rows // 8, 8, channels), axis=0)


def dot_first(a, b):
    return lax.dot_general(a, b, (((0,), (0,)), ((), ())), preferred_element_type=F32)


def dot_last(a, b):
    return lax.dot_general(a, b, (((1,), (1,)), ((), ())), preferred_element_type=F32)


def kernel(
    ns, nz, parts, early,
    wave_in, lengths_in, conv_one_in, conv_two_in, gain_one_in, shift_one_in, gain_two_in, shift_two_in, cot_in,
    features, grad_one_out, grad_two_out, norms_out,
    wave, lengths, conv_one, conv_two, gain_one, shift_one, gain_two, shift_two, cot, in_s,
    halo, patch, pre, hat, inv, phi, even, patch_two, pre_two, dpre_two, dpre_far, shifted, dact, dhi, dlo,
    order, cot_rows, feat, select,
    mine, from_seq, seq_sum, from_z, from_early, early_sum, from_late, full,
    small, small_core, small_sum, small_seq, small_part, small_z, small_all,
    halo_s, halo_r, p_s, p_r, a_s, a_r, b_s, b_r, c_s, c_r, d_s, d_r, e_s, e_r, x_s, x_r,
    sa_s, sa_r, sb_s, sb_r, sc_s, sc_r, sd_s, sd_r,
):
    clips, samples = wave.shape
    channels = conv_two.shape[1]
    half = samples // (2 * TAPS // 2)
    rows = clips * half
    middle = channels // 2
    block = mine.shape[1]

    pos = lax.axis_index("seq")
    dp = lax.axis_index("dp")
    z, core = dp // 2, lax.rem(dp, 2)
    partner = dp + 1 - 2 * core

    def at(dp_index, seq_index):
        return {"device_id": (dp_index, seq_index), "device_id_type": MESH}

    def seq_peer(d):
        return lax.rem(pos + d, ns)

    def z_peer(d):
        return lax.rem(z + d, nz)

    loads = [
        pltpu.make_async_copy(source, target, in_s.at[i])
        for i, (source, target) in enumerate(
            (
                (wave_in, wave),
                (conv_one_in, conv_one),
                (gain_one_in, gain_one),
                (shift_one_in, shift_one),
                (lengths_in, lengths),
                (cot_in, cot),
                (gain_two_in, gain_two),
                (shift_two_in, shift_two),
                (conv_two_in, conv_two),
            )
        )
    ]
    for load in loads[:4]:
        load.start()
    barrier = pltpu.get_barrier_semaphore()
    for d in range(1, nz):
        pl.semaphore_signal(barrier, inc=1, **at(2 * z_peer(d) + core, pos))
        pl.semaphore_signal(barrier, inc=1, **at(2 * z_peer(d) + 1 - core, pos))
    for d in range(1, ns):
        pl.semaphore_signal(barrier, inc=1, **at(dp, seq_peer(d)))
    pl.semaphore_signal(barrier, inc=1, **at(partner, pos))
    for load in loads[4:]:
        load.start()

    def iota(shape, dim):
        return lax.broadcasted_iota(jnp.int32, shape, dim)

    sample = iota((samples, 128), 0)
    tap_of = sample - TAPS * lax.shift_right_logical(sample * TENTH, 16)
    column = iota((8, 128), 1)
    for parity in range(2):
        wanted = lax.rem(column + parity * TAPS // 2, TAPS)
        wanted = jnp.where(column < 3 * TAPS, wanted, -1)[0:1]
        select[parity] = jnp.where(tap_of == wanted, 1.0, 0.0).astype(BF16)

    for load in loads[:4]:
        load.wait()
    g1, b1 = gain_one[...], shift_one[...]
    taps = conv_one[...].astype(F32)
    taps = taps - jnp.mean(taps, axis=-1, keepdims=True)
    high = taps.astype(BF16).astype(F32)
    middling = (taps - high).astype(BF16).astype(F32)
    low = taps - high - middling
    thirds = jnp.concatenate([high, middling, low], axis=0).astype(BF16)
    wave_f = wave[...].astype(F32)
    spread = jnp.concatenate([wave_f] * (rows // clips), axis=0)
    lane = iota((rows, samples), 1) - TAPS * lax.div(iota((rows, samples), 0), clips)
    for parity in range(2):
        offset = parity * TAPS // 2
        hit = (lane >= offset) & (lane < offset + TAPS)
        picked = jnp.where(hit, spread, 0.0).astype(BF16)
        found = jnp.dot(picked, select[parity], preferred_element_type=F32)
        patch[parity * rows : (parity + 1) * rows] = found
        pre[parity * rows : (parity + 1) * rows] = jnp.dot(
            found.astype(BF16)[:, 0 : 3 * TAPS], thirds, preferred_element_type=F32
        )

    def forward_one(value):
        normed, inverse = scale_norm(value)
        out = normed * g1 + b1
        probability, _ = cdf_and_bell(out)
        return normed, inverse, probability, out * probability

    def first_rows(r):
        normed, inverse, probability, act = forward_one(pre[pl.ds(r, STEP)])
        hat[pl.ds(r, STEP)] = normed
        inv[pl.ds(r, STEP)] = jnp.broadcast_to(inverse, (STEP, 128))
        phi[pl.ds(r, STEP)] = probability
        return act

    def even_rows(i):
        r = pl.multiple_of(i * STEP, STEP)
        act = first_rows(r)
        even[pl.ds(r, STEP)] = act
        patch_two[pl.ds(r, STEP), pl.ds(0, channels)] = act.astype(BF16)

    def odd_rows(i):
        r = pl.multiple_of(i * STEP, STEP)
        act = first_rows(pl.multiple_of(rows + r, STEP))
        patch_two[pl.ds(r, STEP), pl.ds(channels, channels)] = act.astype(BF16)

    blocks = rows // STEP
    pl.loop(0, blocks, unroll=UNROLL)(even_rows)
    pl.semaphore_wait(barrier, ns + 2 * (nz - 1))
    halo_copy = pltpu.make_async_remote_copy(
        wave.at[:, pl.ds(0, 128)], halo, halo_s, halo_r, **at(dp, lax.rem(pos + ns - 1, ns))
    )
    halo_copy.start()

    pl.loop(0, blocks - 1, unroll=UNROLL)(odd_rows)

    for load in loads[4:6]:
        load.wait()
    clip_of = lax.rem(iota((rows, rows), 0), clips)
    frame_of = lax.div(iota((rows, rows), 0), clips)
    limit = jnp.full((rows, rows), lengths[0, 0] // TAPS - 1, jnp.int32)
    for c in range(1, clips):
        limit = jnp.where(clip_of == c, lengths[0, c] // TAPS - 1, limit)
    order[...] = jnp.where(
        (iota((rows, rows), 1) == clip_of * half + frame_of) & (pos * half + frame_of < limit), 1.0, 0.0
    ).astype(BF16)
    cot_rows[...] = jnp.dot(order[...], cot[...], preferred_element_type=F32)

    inside = jnp.where(pos < ns - 1, 1.0, 0.0).astype(F32)
    last = 2 * rows - clips
    late = jnp.concatenate([taps[TAPS // 2 : TAPS], jnp.zeros((TAPS // 2, channels), F32)], axis=0)
    both = jnp.concatenate([taps, late], axis=1)
    both_high = both.astype(BF16)
    both_rest = both - both_high.astype(F32)
    both_middle = both_rest.astype(BF16)
    both_low = (both_rest - both_middle.astype(F32)).astype(BF16)
    halo_copy.wait_recv()
    edge = (halo[...].astype(F32) * inside).astype(BF16)
    edges = sum(
        jnp.dot(edge[:, 0:TAPS], part, preferred_element_type=F32)
        for part in (both_low, both_middle, both_high)
    )
    pre[last : last + clips] = pre[last : last + clips] + edges[:, channels : 2 * channels]
    edge_hat, edge_inv, edge_phi, edge_act = forward_one(edges[:, 0:channels])
    even[rows : rows + clips] = edge_act * inside
    odd_rows(blocks - 1)
    patch_two[0:rows, 2 * channels : 3 * channels] = even[clips : clips + rows].astype(BF16)
    patch_copy = pltpu.make_async_remote_copy(
        patch_two.at[pl.ds(0, rows)], patch_two.at[pl.ds(rows, rows)], p_s, p_r, **at(partner, pos)
    )

    def dpre_copy(which):
        part = pl.ds(which * (rows // 2), rows // 2)
        return pltpu.make_async_remote_copy(
            dpre_two.at[1 - core, part], dpre_far.at[part], a_s.at[which], a_r.at[which], **at(partner, pos)
        )

    patch_copy.start()

    for load in loads[6:]:
        load.wait()
    g2, b2 = gain_two[...], shift_two[...]
    pre_two[...] = jnp.dot(patch_two[0:rows], conv_two[...], preferred_element_type=F32)

    zeros8 = jnp.zeros((8, channels), F32)

    def second(i, sums):
        r = pl.multiple_of(i * STEP, STEP)
        normed, inverse = layer_norm(pre_two[pl.ds(r, STEP)])
        out = normed * g2 + b2
        probability, bell = cdf_and_bell(out)
        feat[pl.ds(r, STEP)] = (out * probability).astype(BF16)
        up = cot_rows[pl.ds(r, STEP)] * (probability + out * bell * normal_peak)
        down = norm_backward(up, normed, inverse, g2).astype(BF16)
        dpre_two[0, pl.ds(r, STEP)] = down[:, 0:middle]
        dpre_two[1, pl.ds(r, STEP)] = down[:, middle:channels]
        return sums[0] + fold8(up * normed), sums[1] + fold8(up)

    sums_two = lax.fori_loop(0, blocks // 2, second, (zeros8, zeros8), unroll=UNROLL)
    dpre_copy(0).start()
    two_hat, two_up = lax.fori_loop(blocks // 2, blocks, second, sums_two, unroll=UNROLL)
    dpre_copy(1).start()

    def back_dot(first):
        return dot_last(dpre_two[0], conv_two[first : first + channels, 0:middle]) + dot_last(
            dpre_two[1], conv_two[first : first + channels, middle:channels]
        )

    shifted[0:8] = jnp.zeros((8, channels), F32)
    shifted[8 : 8 + rows] = back_dot(2 * channels)
    dact[0:rows] = back_dot(0) + shifted[8 - clips : 8 - clips + rows]
    dact[rows : 2 * rows] = back_dot(channels)

    def seq_copy(q, d):
        start, count = parts[q]
        b = seq_peer(d)
        return pltpu.make_async_remote_copy(
            mine.at[b, pl.ds(start, count)], from_seq.at[d - 1, pl.ds(start, count)],
            b_s.at[q, d - 1], b_r.at[q, d - 1], **at(dp, b),
        )

    def pieces_of(q):
        return min(nz, parts[q][1] // 16)

    def z_rows(q, owner):
        piece = parts[q][1] // pieces_of(q)
        return pl.ds(pl.multiple_of(parts[q][0] + owner * piece, 16), piece)

    def z_copy(q, d):
        piece = parts[q][1] // pieces_of(q)
        return pltpu.make_async_remote_copy(
            seq_sum.at[z_rows(q, z_peer(d))], from_z.at[q, d - 1, pl.ds(0, piece)],
            c_s.at[q, d - 1], c_r.at[q, d - 1], **at(2 * z_peer(d) + core, pos),
        )

    def spread_copy(q, d):
        there = full.at[core, z_rows(q, z)]
        return pltpu.make_async_remote_copy(
            there, there, d_s.at[q, d - 1], d_r.at[q, d - 1], **at(2 * z_peer(d) + core, pos)
        )

    def cross_copy(q, d):
        there = full.at[core, z_rows(q, z)]
        return pltpu.make_async_remote_copy(
            there, there, x_s.at[d], x_r.at[d], **at(2 * z_peer(d) + 1 - core, pos)
        )

    def cross_copy_from(q, d):
        there = full.at[1 - core, z_rows(q, z_peer(nz - d))]
        return pltpu.make_async_remote_copy(
            there, there, x_s.at[d], x_r.at[d], **at(2 * z_peer(d) + 1 - core, pos)
        )

    def spread_copy_from(q, d):
        there = full.at[core, z_rows(q, z_peer(nz - d))]
        return pltpu.make_async_remote_copy(
            there, there, d_s.at[q, d - 1], d_r.at[q, d - 1], **at(2 * z_peer(d) + core, pos)
        )

    def part_rows(q):
        return pl.ds(parts[q][0], parts[q][1])

    def early_copy(q, d):
        return pltpu.make_async_remote_copy(
            mine.at[:, z_rows(q, z_peer(d))], from_early.at[d - 1],
            c_s.at[q, d - 1], c_r.at[q, d - 1], **at(2 * z_peer(d) + core, pos),
        )

    def late_copy(q, d):
        return pltpu.make_async_remote_copy(
            early_sum.at[seq_peer(d)], from_late.at[d - 1],
            b_s.at[q, d - 1], b_r.at[q, d - 1], **at(dp, seq_peer(d)),
        )

    def relay_copy(q, which):
        there = full.at[which, part_rows(q)]
        return pltpu.make_async_remote_copy(there, there, e_s.at[q], e_r.at[q], **at(partner, pos))

    def when_owner(q, owner, action):
        if pieces_of(q) == nz:
            action()
        else:
            pl.when(owner < pieces_of(q))(action)

    near = dpre_two[core]
    features[...] = dot_first(order[...], feat[...]).astype(BF16)
    patch_copy.wait_recv()
    for which in range(2):
        dpre_copy(which).wait_recv()
    down = jnp.concatenate([near, dpre_far[...]], axis=0)
    def start_early(q):
        for d in range(1, nz):
            when_owner(q, z_peer(d), lambda d=d: early_copy(q, d).start())

    if block % 128 == 0:
        own = []
        for q in sorted(range(len(parts)), key=lambda q: q not in early):
            start, size = parts[q]
            for d in range(1, ns + 1):
                b = seq_peer(d)
                for first in range(start, start + size, 128):
                    columns = pl.ds(pl.multiple_of(b * block + first, 128), 128)

                    def multiply(b=b, first=first, columns=columns):
                        mine[b, first : first + 128] = dot_first(patch_two[:, columns], down).astype(BF16)

                    if d == ns and q not in early:
                        own.append(multiply)
                    else:
                        multiply()
                if d < ns and q not in early:
                    seq_copy(q, d).start()
            if q in early:
                start_early(q)
        for multiply in own:
            multiply()
    else:
        group = 384
        for i in range(3 * channels // group):
            product = dot_first(patch_two[:, i * group : (i + 1) * group], down).astype(BF16)
            for j in range(group // block):
                mine[i * (group // block) + j] = product[j * block : (j + 1) * block]
        for q in range(len(parts)):
            if q in early:
                start_early(q)
            else:
                for d in range(1, ns):
                    seq_copy(q, d).start()

    def backward_one(incoming, normed, inverse, probability):
        up = incoming * slope_of(normed * g1 + b1, probability)
        return up, norm_backward(up, normed, inverse, g1)

    def back(i, sums):
        at_rows = pl.ds(pl.multiple_of(i * STEP, STEP), STEP)
        normed = hat[at_rows]
        up, dpre = backward_one(dact[at_rows], normed, inv[at_rows, 0:1], phi[at_rows])
        high = dpre.astype(BF16)
        dhi[at_rows] = high
        dlo[at_rows] = (dpre - high.astype(F32)).astype(BF16)
        return sums[0] + fold8(up * normed), sums[1] + fold8(up)

    one_hat, one_up = lax.fori_loop(0, 2 * rows // STEP, back, (zeros8, zeros8), unroll=UNROLL)

    edge_in = shifted[8 + rows - clips : 8 + rows] * inside
    edge_up, edge_dpre = backward_one(edge_in, edge_hat, edge_inv, edge_phi)
    edge_high = edge_dpre.astype(BF16)
    edge_low = (edge_dpre - edge_high.astype(F32)).astype(BF16)

    moved = iota((128, 128), 0) + TAPS // 2
    tap = iota((128, 128), 1)
    fix = jnp.dot(
        edge, jnp.where((moved == tap) & (tap < TAPS), 1.0, 0.0).astype(BF16), preferred_element_type=F32
    )
    patch[last : last + clips] = patch[last : last + clips] + fix
    frames = patch[...].astype(BF16)
    grad_one = (
        dot_first(frames, dhi[...])
        + dot_first(frames, dlo[...])
    )[0:16] + (dot_first(edge, edge_high) + dot_first(edge, edge_low))[0:16]

    def total_row(value):
        return jnp.sum(value, axis=0, keepdims=True)

    sums = (
        (0, grad_one),
        (10, total_row(one_hat) + total_row(edge_up * edge_hat)),
        (11, total_row(one_up) + total_row(edge_up)),
        (12, total_row(two_hat)),
        (13, total_row(two_up)),
        (14, jnp.zeros((2, channels), F32)),
    )
    for row, value in sums:
        for h in range(2):
            small[h, row : row + value.shape[0]] = value[:, h * middle : (h + 1) * middle]

    small_core_copy = pltpu.make_async_remote_copy(
        small.at[1 - core], small_core, sa_s, sa_r, **at(partner, pos)
    )
    small_core_copy.start()

    def small_seq_copy(d):
        return pltpu.make_async_remote_copy(
            small_sum, small_seq.at[pos], sb_s.at[d - 1], sb_r.at[d - 1], **at(dp, seq_peer(d))
        )

    def small_z_copy(d):
        return pltpu.make_async_remote_copy(
            small_part, small_z.at[z], sc_s.at[d - 1], sc_r.at[d - 1], **at(2 * z_peer(d) + core, pos)
        )

    def small_done_copy(which):
        return pltpu.make_async_remote_copy(
            small_all.at[which], small_all.at[which], sd_s, sd_r, **at(partner, pos)
        )

    def seq_done(q):
        span = pl.ds(parts[q][0], parts[q][1])
        total = mine[pos, span].astype(F32)
        for d in range(1, ns):
            seq_copy(q, d).wait_recv()
            total = total + from_seq[d - 1, span].astype(F32)
        value = total.astype(BF16)
        seq_sum[span] = value
        for d in range(1, nz):
            when_owner(q, z_peer(d), lambda d=d: z_copy(q, d).start())

    def z_done(q):
        def action():
            piece = parts[q][1] // pieces_of(q)
            total = seq_sum[z_rows(q, z)].astype(F32)
            for d in range(1, nz):
                z_copy(q, d).wait_recv()
                total = total + from_z[q, d - 1, pl.ds(0, piece)].astype(F32)
            full[core, z_rows(q, z)] = total.astype(BF16)
            for d in range(1, nz):
                spread_copy(q, d).start()
                if q == CROSSED:
                    cross_copy(q, d).start()
            if q == CROSSED:
                cross_copy(q, 0).start()

        when_owner(q, z, action)

    def early_done(q):
        def action():
            for d in range(1, nz):
                early_copy(q, d).wait_recv()
            for d in [*range(1, ns), 0]:
                b = seq_peer(d)
                total = mine[b, z_rows(q, z)].astype(F32)
                for other in range(nz - 1):
                    total = total + from_early[other, b].astype(F32)
                early_sum[b] = total.astype(BF16)
                if d:
                    late_copy(q, d).start()

        when_owner(q, z, action)

    def late_done(q):
        def action():
            total = early_sum[pos].astype(F32)
            for d in range(1, ns):
                late_copy(q, d).wait_recv()
                total = total + from_late[d - 1].astype(F32)
            full[core, z_rows(q, z)] = total.astype(BF16)
            for d in range(1, nz):
                spread_copy(q, d).start()

        when_owner(q, z, action)

    def relay(q):
        for d in range(1, nz):
            when_owner(q, z_peer(nz - d), lambda d=d: spread_copy_from(q, d).wait_recv())
        if q != CROSSED:
            relay_copy(q, core).start()

    def small_step(step):
        if step == 0:
            small_core_copy.wait_recv()
            value = (small[core] + small_core[...]).astype(BF16)
            small_part[...] = value
            small_z[z] = value
            for d in range(1, nz):
                small_z_copy(d).start()
        elif step == 1:
            for d in range(1, nz):
                small_z_copy(d).wait_recv()
            total = small_z[0].astype(F32)
            for p in range(1, nz):
                total = total + small_z[p].astype(F32)
            value = total.astype(BF16)
            small_sum[...] = value
            small_seq[pos] = value
            for d in range(1, ns):
                small_seq_copy(d).start()
        else:
            for d in range(1, ns):
                small_seq_copy(d).wait_recv()
            total = small_seq[0].astype(F32)
            for p in range(1, ns):
                total = total + small_seq[p].astype(F32)
            small_all[core] = total
            small_done_copy(core).start()

    events = {"s": seq_done, "z": z_done, "f": early_done, "g": late_done, "a": relay, "m": small_step}
    for event in SEQUENCE:
        events[event[0]](int(event[1]))

    small_done_copy(core).wait_send()
    small_done_copy(1 - core).wait_recv()
    for h in range(2):
        grad_one_out[:, h * middle : (h + 1) * middle] = small_all[h, 0:TAPS]
        norms_out[:, h * middle : (h + 1) * middle] = small_all[h, 10:14]

    small_core_copy.wait_send()
    for d in range(1, nz):
        small_z_copy(d).wait_send()
    for d in range(1, ns):
        small_seq_copy(d).wait_send()
    halo_copy.wait_send()
    patch_copy.wait_send()
    for which in range(2):
        dpre_copy(which).wait_send()
    for q in range(len(parts)):
        if q in early:
            for d in range(1, nz):
                when_owner(q, z_peer(d), lambda q=q, d=d: early_copy(q, d).wait_send())
        else:
            for d in range(1, ns):
                seq_copy(q, d).wait_send()
            for d in range(1, nz):
                when_owner(q, z_peer(d), lambda q=q, d=d: z_copy(q, d).wait_send())

        def sent(q=q):
            if q in early:
                for d in range(1, ns):
                    late_copy(q, d).wait_send()
            for d in range(1, nz):
                spread_copy(q, d).wait_send()
            if q == CROSSED:
                for d in range(nz):
                    cross_copy(q, d).wait_send()

        when_owner(q, z, sent)
    for q in [int(event[1]) for event in SEQUENCE if event[0] == "a"]:
        start, size = parts[q]
        grad_two_out[start : start + size, pl.ds(pl.multiple_of(core * middle, 128), middle)] = full[core, part_rows(q)]
        if q == CROSSED:
            for d in range(nz):
                when_owner(q, z_peer(nz - d), lambda d=d: cross_copy_from(q, d).wait_recv())
        else:
            relay_copy(q, core).wait_send()
            relay_copy(q, 1 - core).wait_recv()
        grad_two_out[start : start + size, pl.ds(pl.multiple_of((1 - core) * middle, 128), middle)] = full[
            1 - core, part_rows(q)
        ]


def on_device(ns, nz, waveform, lengths, conv_one, conv_two, gain_one, shift_one, gain_two, shift_two, cotangent):
    clips, samples = waveform.shape
    channels = conv_two.shape[1]
    half = cotangent.shape[1]
    rows = clips * half
    block = conv_two.shape[0] // ns
    unit = block // 6
    parts = tuple(
        (sum(size for size, _ in PLAN[:q]) * unit, size * unit) for q, (size, _) in enumerate(PLAN)
    )
    early = tuple(q for q, (_, over_z) in enumerate(PLAN) if over_z)
    count = len(parts)
    piece = max(size // min(nz, size // 16) for _, size in parts)
    early_piece = max(parts[q][1] // min(nz, parts[q][1] // 16) for q in early)
    middle = channels // 2
    dma = pltpu.SemaphoreType.DMA
    vmem = pl.BlockSpec(memory_space=pltpu.VMEM)
    hbm = pl.BlockSpec(memory_space=pltpu.HBM)
    features, grad_one, grad_two, norms = pl.pallas_call(
        functools.partial(kernel, ns, nz, parts, early),
        out_shape=(
            jax.ShapeDtypeStruct((rows, channels), BF16),
            jax.ShapeDtypeStruct((TAPS, channels), F32),
            jax.ShapeDtypeStruct((block, channels), BF16),
            jax.ShapeDtypeStruct((4, channels), F32),
        ),
        in_specs=[hbm] * 9,
        out_specs=(vmem,) * 4,
        scratch_shapes=[
            pltpu.VMEM(waveform.shape, BF16),
            pltpu.SMEM(lengths.shape, jnp.int32),
            pltpu.VMEM(conv_one.shape, BF16),
            pltpu.VMEM(conv_two.shape, BF16),
            pltpu.VMEM((1, channels), F32),
            pltpu.VMEM((1, channels), F32),
            pltpu.VMEM((1, channels), F32),
            pltpu.VMEM((1, channels), F32),
            pltpu.VMEM((rows, channels), BF16),
            dma((9,)),
            pltpu.VMEM((clips, 128), BF16),
            pltpu.VMEM((2 * rows, 128), F32),
            pltpu.VMEM((2 * rows, channels), F32),
            pltpu.VMEM((2 * rows, channels), F32),
            pltpu.VMEM((2 * rows, 128), F32),
            pltpu.VMEM((2 * rows, channels), F32),
            pltpu.VMEM((rows + 8, channels), F32),
            pltpu.VMEM((2 * rows, 3 * channels), BF16),
            pltpu.VMEM((rows, channels), F32),
            pltpu.VMEM((2, rows, middle), BF16),
            pltpu.VMEM((rows, middle), BF16),
            pltpu.VMEM((rows + 8, channels), F32),
            pltpu.VMEM((2 * rows, channels), F32),
            pltpu.VMEM((2 * rows, channels), BF16),
            pltpu.VMEM((2 * rows, channels), BF16),
            pltpu.VMEM((rows, rows), BF16),
            pltpu.VMEM((rows, channels), F32),
            pltpu.VMEM((rows, channels), BF16),
            pltpu.VMEM((2, samples, 128), BF16),
            pltpu.VMEM((ns, block, middle), BF16),
            pltpu.VMEM((ns - 1, block, middle), BF16),
            pltpu.VMEM((block, middle), BF16),
            pltpu.VMEM((count, nz - 1, piece, middle), BF16),
            pltpu.VMEM((nz - 1, ns, early_piece, middle), BF16),
            pltpu.VMEM((ns, early_piece, middle), BF16),
            pltpu.VMEM((ns - 1, early_piece, middle), BF16),
            pltpu.VMEM((2, block, middle), BF16),
            pltpu.VMEM((2, 16, middle), F32),
            pltpu.VMEM((16, middle), F32),
            pltpu.VMEM((16, middle), BF16),
            pltpu.VMEM((ns, 16, middle), BF16),
            pltpu.VMEM((16, middle), BF16),
            pltpu.VMEM((nz, 16, middle), BF16),
            pltpu.VMEM((2, 16, middle), F32),
            dma, dma,
            dma, dma,
            dma((2,)), dma((2,)),
            dma((count, ns - 1)), dma((count, ns - 1)),
            dma((count, nz - 1)), dma((count, nz - 1)),
            dma((count, nz - 1)), dma((count, nz - 1)),
            dma((count,)), dma((count,)),
            dma((nz,)), dma((nz,)),
            dma, dma,
            dma((ns - 1,)), dma((ns - 1,)),
            dma((nz - 1,)), dma((nz - 1,)),
            dma, dma,
        ],
        compiler_params=pltpu.CompilerParams(
            collective_id=0, has_side_effects=True, vmem_limit_bytes=48 * 1024 * 1024
        ),
    )(
        *[
            pltpu.with_memory_space_constraint(value, pltpu.HBM)
            for value in (
        waveform,
        lengths,
        conv_one,
        conv_two,
        gain_one.reshape(1, channels),
        shift_one.reshape(1, channels),
        gain_two.reshape(1, channels),
        shift_two.reshape(1, channels),
        cotangent.reshape(rows, channels),
    )])
    features, grad_one, grad_two, norms = pl.pallas_call(
        put_out,
        out_shape=(
            jax.ShapeDtypeStruct((rows, channels), BF16),
            jax.ShapeDtypeStruct((TAPS, channels), F32),
            jax.ShapeDtypeStruct((block, channels), F32),
            jax.ShapeDtypeStruct((4, channels), F32),
        ),
        in_specs=[vmem] * 4,
        out_specs=(hbm,) * 4,
        scratch_shapes=[pltpu.VMEM((block, channels), F32), dma((6,))],
        compiler_params=pltpu.CompilerParams(vmem_limit_bytes=4 * 1024 * 1024),
    )(features, grad_one, grad_two, norms)
    return features.reshape(clips, half, channels), grad_one, grad_two, norms


def put_out(features, grad_one, grad_two, norms, features_out, grad_one_out, grad_two_out, norms_out, wide, sem):
    rows = wide.shape[0] // 3
    copies = [
        pltpu.make_async_copy(source, target, sem.at[i])
        for i, (source, target) in enumerate(
            ((features, features_out), (grad_one, grad_one_out), (norms, norms_out))
        )
    ]
    for copy in copies:
        copy.start()
    for i in range(3):
        part = pl.ds(i * rows, rows)
        wide[part] = grad_two[part].astype(F32)
        copies.append(pltpu.make_async_copy(wide.at[part], grad_two_out.at[part], sem.at[3 + i]))
        copies[-1].start()
    for copy in copies:
        copy.wait()


def solution(mesh):
    in_specs = (P("dp", "seq"), P("dp", None), P(), P(), P(), P(), P(), P(), P("dp", "seq", None))
    out_specs = (P("dp", "seq", None), P(), P("seq", None), P())
    return jax.shard_map(
        functools.partial(on_device, mesh.shape["seq"], mesh.shape["dp"] // 2),
        mesh=mesh, in_specs=in_specs, out_specs=out_specs, check_vma=False,
    )
```

```python
import functools

import jax
import jax.numpy as jnp
from jax import lax
from jax.experimental import pallas as pl
from jax.experimental.pallas import tpu as pltpu
from jax.sharding import PartitionSpec as P

MESH = pl.DeviceIdType.MESH
F32, BF16 = jnp.float32, jnp.bfloat16

epsilon = 1e-05
root_half = 0.7071067811865476
normal_peak = 0.3989422804014327

TAPS = 10
TENTH = 6554
STEP = 16
UNROLL = 8
PLAN = ((2, False), (2, False), (2, True))
CROSSED = 1
SEQUENCE = ('m0', 's0', 'f2', 's1', 'm1', 'z0', 'g2', 'z1', 'm2', 'a0', 'a2', 'a1')


def half_erfc_terms():
    scaled = (0.254829592, -0.284496736, 1.421413741, -1.453152027, 1.061405429)
    return [0.5 * term for term in scaled]


def cdf_and_bell(values):
    t = pltpu.reciprocal(1.0 + 0.3275911 * root_half * jnp.abs(values), approx=True)
    bell = jnp.exp(-0.5 * values * values)
    c1, c2, c3, c4, c5 = half_erfc_terms()
    tail = t * (c1 + t * (c2 + t * (c3 + t * (c4 + t * c5)))) * bell
    return jnp.where(values >= 0.0, 1.0 - tail, tail), bell


def slope_of(values, phi):
    return phi + values * jnp.exp(-0.5 * values * values) * normal_peak


def scale_norm(centre):
    inverse = lax.rsqrt(jnp.mean(centre * centre, axis=-1, keepdims=True) + epsilon)
    return centre * inverse, inverse


def layer_norm(pre):
    return scale_norm(pre - jnp.mean(pre, axis=-1, keepdims=True))


def norm_backward(upstream, normed, inverse, gain):
    scaled = upstream * gain
    return inverse * (
        scaled
        - jnp.mean(scaled, axis=-1, keepdims=True)
        - normed * jnp.mean(scaled * normed, axis=-1, keepdims=True)
    )


def fold8(value):
    rows, channels = value.shape
    return jnp.sum(value.reshape(rows // 8, 8, channels), axis=0)


def dot_first(a, b):
    return lax.dot_general(a, b, (((0,), (0,)), ((), ())), preferred_element_type=F32)


def dot_last(a, b):
    return lax.dot_general(a, b, (((1,), (1,)), ((), ())), preferred_element_type=F32)


def kernel(
    ns, nz, parts, early,
    wave_in, lengths_in, conv_one_in, conv_two_in, gain_one_in, shift_one_in, gain_two_in, shift_two_in, cot_in,
    features, grad_one_out, grad_two_out, norms_out,
    wave, lengths, conv_one, conv_two, gain_one, shift_one, gain_two, shift_two, cot, in_s,
    halo, patch, pre, hat, inv, phi, even, patch_two, pre_two, dpre_two, dpre_far, shifted, dact, dhi, dlo,
    order, cot_rows, feat, select,
    near_product, mine, from_seq, seq_sum, from_z, from_early, early_sum, from_late, full,
    small, small_core, small_sum, small_seq, small_part, small_z, small_all,
    halo_s, halo_r, p_s, p_r, a_s, a_r, b_s, b_r, c_s, c_r, d_s, d_r, e_s, e_r, x_s, x_r,
    sa_s, sa_r, sb_s, sb_r, sc_s, sc_r, sd_s, sd_r,
):
    clips, samples = wave.shape
    channels = conv_two.shape[1]
    half = samples // (2 * TAPS // 2)
    rows = clips * half
    middle = channels // 2
    block = mine.shape[1]

    pos = lax.axis_index("seq")
    dp = lax.axis_index("dp")
    z, core = dp // 2, lax.rem(dp, 2)
    partner = dp + 1 - 2 * core

    def at(dp_index, seq_index):
        return {"device_id": (dp_index, seq_index), "device_id_type": MESH}

    def seq_peer(d):
        return lax.rem(pos + d, ns)

    def z_peer(d):
        return lax.rem(z + d, nz)

    loads = [
        pltpu.make_async_copy(source, target, in_s.at[i])
        for i, (source, target) in enumerate(
            (
                (wave_in, wave),
                (conv_one_in, conv_one),
                (gain_one_in, gain_one),
                (shift_one_in, shift_one),
                (lengths_in, lengths),
                (cot_in, cot),
                (gain_two_in, gain_two),
                (shift_two_in, shift_two),
                (conv_two_in, conv_two),
            )
        )
    ]
    for load in loads[:4]:
        load.start()
    barrier = pltpu.get_barrier_semaphore()
    for d in range(1, nz):
        pl.semaphore_signal(barrier, inc=1, **at(2 * z_peer(d) + core, pos))
        pl.semaphore_signal(barrier, inc=1, **at(2 * z_peer(d) + 1 - core, pos))
    for d in range(1, ns):
        pl.semaphore_signal(barrier, inc=1, **at(dp, seq_peer(d)))
    pl.semaphore_signal(barrier, inc=1, **at(partner, pos))
    for load in loads[4:]:
        load.start()

    def iota(shape, dim):
        return lax.broadcasted_iota(jnp.int32, shape, dim)

    sample = iota((samples, 128), 0)
    tap_of = sample - TAPS * lax.shift_right_logical(sample * TENTH, 16)
    column = iota((8, 128), 1)
    for parity in range(2):
        wanted = lax.rem(column + parity * TAPS // 2, TAPS)
        wanted = jnp.where(column < 3 * TAPS, wanted, -1)[0:1]
        select[parity] = jnp.where(tap_of == wanted, 1.0, 0.0).astype(BF16)

    for load in loads[:4]:
        load.wait()
    g1, b1 = gain_one[...], shift_one[...]
    taps = conv_one[...].astype(F32)
    taps = taps - jnp.mean(taps, axis=-1, keepdims=True)
    high = taps.astype(BF16).astype(F32)
    middling = (taps - high).astype(BF16).astype(F32)
    low = taps - high - middling
    thirds = jnp.concatenate([high, middling, low], axis=0).astype(BF16)
    wave_f = wave[...].astype(F32)
    spread = jnp.concatenate([wave_f] * (rows // clips), axis=0)
    lane = iota((rows, samples), 1) - TAPS * lax.div(iota((rows, samples), 0), clips)
    for parity in range(2):
        offset = parity * TAPS // 2
        hit = (lane >= offset) & (lane < offset + TAPS)
        picked = jnp.where(hit, spread, 0.0).astype(BF16)
        found = jnp.dot(picked, select[parity], preferred_element_type=F32)
        patch[parity * rows : (parity + 1) * rows] = found
        pre[parity * rows : (parity + 1) * rows] = jnp.dot(
            found.astype(BF16)[:, 0 : 3 * TAPS], thirds, preferred_element_type=F32
        )

    def forward_one(value):
        normed, inverse = scale_norm(value)
        out = normed * g1 + b1
        probability, _ = cdf_and_bell(out)
        return normed, inverse, probability, out * probability

    def first_rows(r):
        normed, inverse, probability, act = forward_one(pre[pl.ds(r, STEP)])
        hat[pl.ds(r, STEP)] = normed
        inv[pl.ds(r, STEP)] = jnp.broadcast_to(inverse, (STEP, 128))
        phi[pl.ds(r, STEP)] = probability
        return act

    def even_rows(i):
        r = pl.multiple_of(i * STEP, STEP)
        act = first_rows(r)
        even[pl.ds(r, STEP)] = act
        patch_two[pl.ds(r, STEP), pl.ds(0, channels)] = act.astype(BF16)

    def odd_rows(i):
        r = pl.multiple_of(i * STEP, STEP)
        act = first_rows(pl.multiple_of(rows + r, STEP))
        patch_two[pl.ds(r, STEP), pl.ds(channels, channels)] = act.astype(BF16)

    blocks = rows // STEP
    pl.loop(0, blocks, unroll=UNROLL)(even_rows)
    pl.semaphore_wait(barrier, ns + 2 * (nz - 1))
    halo_copy = pltpu.make_async_remote_copy(
        wave.at[:, pl.ds(0, 128)], halo, halo_s, halo_r, **at(dp, lax.rem(pos + ns - 1, ns))
    )
    halo_copy.start()

    pl.loop(0, blocks - 1, unroll=UNROLL)(odd_rows)

    for load in loads[4:6]:
        load.wait()
    clip_of = lax.rem(iota((rows, rows), 0), clips)
    frame_of = lax.div(iota((rows, rows), 0), clips)
    limit = jnp.full((rows, rows), lengths[0, 0] // TAPS - 1, jnp.int32)
    for c in range(1, clips):
        limit = jnp.where(clip_of == c, lengths[0, c] // TAPS - 1, limit)
    order[...] = jnp.where(
        (iota((rows, rows), 1) == clip_of * half + frame_of) & (pos * half + frame_of < limit), 1.0, 0.0
    ).astype(BF16)
    cot_rows[...] = jnp.dot(order[...], cot[...], preferred_element_type=F32)

    inside = jnp.where(pos < ns - 1, 1.0, 0.0).astype(F32)
    last = 2 * rows - clips
    late = jnp.concatenate([taps[TAPS // 2 : TAPS], jnp.zeros((TAPS // 2, channels), F32)], axis=0)
    both = jnp.concatenate([taps, late], axis=1)
    both_high = both.astype(BF16)
    both_rest = both - both_high.astype(F32)
    both_middle = both_rest.astype(BF16)
    both_low = (both_rest - both_middle.astype(F32)).astype(BF16)
    halo_copy.wait_recv()
    edge = (halo[...].astype(F32) * inside).astype(BF16)
    edges = sum(
        jnp.dot(edge[:, 0:TAPS], part, preferred_element_type=F32)
        for part in (both_low, both_middle, both_high)
    )
    pre[last : last + clips] = pre[last : last + clips] + edges[:, channels : 2 * channels]
    edge_hat, edge_inv, edge_phi, edge_act = forward_one(edges[:, 0:channels])
    even[rows : rows + clips] = edge_act * inside
    odd_rows(blocks - 1)
    patch_two[0:rows, 2 * channels : 3 * channels] = even[clips : clips + rows].astype(BF16)
    patch_copy = pltpu.make_async_remote_copy(
        patch_two.at[pl.ds(0, rows)], patch_two.at[pl.ds(rows, rows)], p_s, p_r, **at(partner, pos)
    )

    def dpre_copy(which):
        part = pl.ds(which * (rows // 2), rows // 2)
        return pltpu.make_async_remote_copy(
            dpre_two.at[1 - core, part], dpre_far.at[part], a_s.at[which], a_r.at[which], **at(partner, pos)
        )

    patch_copy.start()

    for load in loads[6:]:
        load.wait()
    g2, b2 = gain_two[...], shift_two[...]
    pre_two[...] = jnp.dot(patch_two[0:rows], conv_two[...], preferred_element_type=F32)

    zeros8 = jnp.zeros((8, channels), F32)

    def second(i, sums):
        r = pl.multiple_of(i * STEP, STEP)
        normed, inverse = layer_norm(pre_two[pl.ds(r, STEP)])
        out = normed * g2 + b2
        probability, bell = cdf_and_bell(out)
        feat[pl.ds(r, STEP)] = (out * probability).astype(BF16)
        up = cot_rows[pl.ds(r, STEP)] * (probability + out * bell * normal_peak)
        down = norm_backward(up, normed, inverse, g2).astype(BF16)
        dpre_two[0, pl.ds(r, STEP)] = down[:, 0:middle]
        dpre_two[1, pl.ds(r, STEP)] = down[:, middle:channels]
        return sums[0] + fold8(up * normed), sums[1] + fold8(up)

    sums_two = lax.fori_loop(0, blocks // 2, second, (zeros8, zeros8), unroll=UNROLL)
    dpre_copy(0).start()
    two_hat, two_up = lax.fori_loop(blocks // 2, blocks, second, sums_two, unroll=UNROLL)
    dpre_copy(1).start()

    def back_dot(first):
        return dot_last(dpre_two[0], conv_two[first : first + channels, 0:middle]) + dot_last(
            dpre_two[1], conv_two[first : first + channels, middle:channels]
        )

    shifted[0:8] = jnp.zeros((8, channels), F32)
    shifted[8 : 8 + rows] = back_dot(2 * channels)
    dact[0:rows] = back_dot(0) + shifted[8 - clips : 8 - clips + rows]
    dact[rows : 2 * rows] = back_dot(channels)

    def seq_copy(q, d):
        start, count = parts[q]
        b = seq_peer(d)
        return pltpu.make_async_remote_copy(
            mine.at[b, pl.ds(start, count)], from_seq.at[d - 1, pl.ds(start, count)],
            b_s.at[q, d - 1], b_r.at[q, d - 1], **at(dp, b),
        )

    def pieces_of(q):
        return min(nz, parts[q][1] // 16)

    def z_rows(q, owner):
        piece = parts[q][1] // pieces_of(q)
        return pl.ds(pl.multiple_of(parts[q][0] + owner * piece, 16), piece)

    def z_copy(q, d):
        piece = parts[q][1] // pieces_of(q)
        return pltpu.make_async_remote_copy(
            seq_sum.at[z_rows(q, z_peer(d))], from_z.at[q, d - 1, pl.ds(0, piece)],
            c_s.at[q, d - 1], c_r.at[q, d - 1], **at(2 * z_peer(d) + core, pos),
        )

    def spread_copy(q, d):
        there = full.at[core, z_rows(q, z)]
        return pltpu.make_async_remote_copy(
            there, there, d_s.at[q, d - 1], d_r.at[q, d - 1], **at(2 * z_peer(d) + core, pos)
        )

    def cross_copy(q, d):
        there = full.at[core, z_rows(q, z)]
        return pltpu.make_async_remote_copy(
            there, there, x_s.at[d], x_r.at[d], **at(2 * z_peer(d) + 1 - core, pos)
        )

    def cross_copy_from(q, d):
        there = full.at[1 - core, z_rows(q, z_peer(nz - d))]
        return pltpu.make_async_remote_copy(
            there, there, x_s.at[d], x_r.at[d], **at(2 * z_peer(d) + 1 - core, pos)
        )

    def spread_copy_from(q, d):
        there = full.at[core, z_rows(q, z_peer(nz - d))]
        return pltpu.make_async_remote_copy(
            there, there, d_s.at[q, d - 1], d_r.at[q, d - 1], **at(2 * z_peer(d) + core, pos)
        )

    def part_rows(q):
        return pl.ds(parts[q][0], parts[q][1])

    def early_copy(q, d):
        return pltpu.make_async_remote_copy(
            mine.at[:, z_rows(q, z_peer(d))], from_early.at[d - 1],
            c_s.at[q, d - 1], c_r.at[q, d - 1], **at(2 * z_peer(d) + core, pos),
        )

    def late_copy(q, d):
        return pltpu.make_async_remote_copy(
            early_sum.at[seq_peer(d)], from_late.at[d - 1],
            b_s.at[q, d - 1], b_r.at[q, d - 1], **at(dp, seq_peer(d)),
        )

    def relay_copy(q, which):
        there = full.at[which, part_rows(q)]
        return pltpu.make_async_remote_copy(there, there, e_s.at[q], e_r.at[q], **at(partner, pos))

    def when_owner(q, owner, action):
        if pieces_of(q) == nz:
            action()
        else:
            pl.when(owner < pieces_of(q))(action)

    near = dpre_two[core]
    features[...] = dot_first(order[...], feat[...]).astype(BF16)
    if block % 128 == 0:
        for q in early:
            for b in range(ns):
                for first in range(0, parts[q][1], 128):
                    columns = pl.ds(b * block + parts[q][0] + first, 128)
                    near_product[b, first : first + 128] = dot_first(patch_two[0:rows, columns], near)
    patch_copy.wait_recv()
    for which in range(2):
        dpre_copy(which).wait_recv()
    down = jnp.concatenate([near, dpre_far[...]], axis=0)
    def start_early(q):
        for d in range(1, nz):
            when_owner(q, z_peer(d), lambda d=d: early_copy(q, d).start())

    if block % 128 == 0:
        own = []
        for q in sorted(range(len(parts)), key=lambda q: q not in early):
            start, size = parts[q]
            for d in range(1, ns + 1):
                b = seq_peer(d)
                for first in range(start, start + size, 128):
                    columns = pl.ds(pl.multiple_of(b * block + first, 128), 128)

                    def multiply(b=b, first=first, columns=columns, q=q):
                        if q in early:
                            far = dot_first(patch_two[rows : 2 * rows, columns], dpre_far[...])
                            product = near_product[b, first - parts[q][0] : first - parts[q][0] + 128] + far
                        else:
                            product = dot_first(patch_two[:, columns], down)
                        mine[b, first : first + 128] = product.astype(BF16)

                    if d == ns and q not in early:
                        own.append(multiply)
                    else:
                        multiply()
                if d < ns and q not in early:
                    seq_copy(q, d).start()
            if q in early:
                start_early(q)
        for multiply in own:
            multiply()
    else:
        group = 384
        for i in range(3 * channels // group):
            product = dot_first(patch_two[:, i * group : (i + 1) * group], down).astype(BF16)
            for j in range(group // block):
                mine[i * (group // block) + j] = product[j * block : (j + 1) * block]
        for q in range(len(parts)):
            if q in early:
                start_early(q)
            else:
                for d in range(1, ns):
                    seq_copy(q, d).start()

    def backward_one(incoming, normed, inverse, probability):
        up = incoming * slope_of(normed * g1 + b1, probability)
        return up, norm_backward(up, normed, inverse, g1)

    def back(i, sums):
        at_rows = pl.ds(pl.multiple_of(i * STEP, STEP), STEP)
        normed = hat[at_rows]
        up, dpre = backward_one(dact[at_rows], normed, inv[at_rows, 0:1], phi[at_rows])
        high = dpre.astype(BF16)
        dhi[at_rows] = high
        dlo[at_rows] = (dpre - high.astype(F32)).astype(BF16)
        return sums[0] + fold8(up * normed), sums[1] + fold8(up)

    one_hat, one_up = lax.fori_loop(0, 2 * rows // STEP, back, (zeros8, zeros8), unroll=UNROLL)

    edge_in = shifted[8 + rows - clips : 8 + rows] * inside
    edge_up, edge_dpre = backward_one(edge_in, edge_hat, edge_inv, edge_phi)
    edge_high = edge_dpre.astype(BF16)
    edge_low = (edge_dpre - edge_high.astype(F32)).astype(BF16)

    moved = iota((128, 128), 0) + TAPS // 2
    tap = iota((128, 128), 1)
    fix = jnp.dot(
        edge, jnp.where((moved == tap) & (tap < TAPS), 1.0, 0.0).astype(BF16), preferred_element_type=F32
    )
    patch[last : last + clips] = patch[last : last + clips] + fix
    frames = patch[...].astype(BF16)
    grad_one = (
        dot_first(frames, dhi[...])
        + dot_first(frames, dlo[...])
    )[0:16] + (dot_first(edge, edge_high) + dot_first(edge, edge_low))[0:16]

    def total_row(value):
        return jnp.sum(value, axis=0, keepdims=True)

    sums = (
        (0, grad_one),
        (10, total_row(one_hat) + total_row(edge_up * edge_hat)),
        (11, total_row(one_up) + total_row(edge_up)),
        (12, total_row(two_hat)),
        (13, total_row(two_up)),
        (14, jnp.zeros((2, channels), F32)),
    )
    for row, value in sums:
        for h in range(2):
            small[h, row : row + value.shape[0]] = value[:, h * middle : (h + 1) * middle]

    small_core_copy = pltpu.make_async_remote_copy(
        small.at[1 - core], small_core, sa_s, sa_r, **at(partner, pos)
    )
    small_core_copy.start()

    def small_seq_copy(d):
        return pltpu.make_async_remote_copy(
            small_sum, small_seq.at[pos], sb_s.at[d - 1], sb_r.at[d - 1], **at(dp, seq_peer(d))
        )

    def small_z_copy(d):
        return pltpu.make_async_remote_copy(
            small_part, small_z.at[z], sc_s.at[d - 1], sc_r.at[d - 1], **at(2 * z_peer(d) + core, pos)
        )

    def small_done_copy(which):
        return pltpu.make_async_remote_copy(
            small_all.at[which], small_all.at[which], sd_s, sd_r, **at(partner, pos)
        )

    def seq_done(q):
        span = pl.ds(parts[q][0], parts[q][1])
        total = mine[pos, span].astype(F32)
        for d in range(1, ns):
            seq_copy(q, d).wait_recv()
            total = total + from_seq[d - 1, span].astype(F32)
        value = total.astype(BF16)
        seq_sum[span] = value
        for d in range(1, nz):
            when_owner(q, z_peer(d), lambda d=d: z_copy(q, d).start())

    def z_done(q):
        def action():
            piece = parts[q][1] // pieces_of(q)
            total = seq_sum[z_rows(q, z)].astype(F32)
            for d in range(1, nz):
                z_copy(q, d).wait_recv()
                total = total + from_z[q, d - 1, pl.ds(0, piece)].astype(F32)
            full[core, z_rows(q, z)] = total.astype(BF16)
            for d in range(1, nz):
                spread_copy(q, d).start()
                if q == CROSSED:
                    cross_copy(q, d).start()
            if q == CROSSED:
                cross_copy(q, 0).start()

        when_owner(q, z, action)

    def early_done(q):
        def action():
            for d in range(1, nz):
                early_copy(q, d).wait_recv()
            for d in [*range(1, ns), 0]:
                b = seq_peer(d)
                total = mine[b, z_rows(q, z)].astype(F32)
                for other in range(nz - 1):
                    total = total + from_early[other, b].astype(F32)
                early_sum[b] = total.astype(BF16)
                if d:
                    late_copy(q, d).start()

        when_owner(q, z, action)

    def late_done(q):
        def action():
            total = early_sum[pos].astype(F32)
            for d in range(1, ns):
                late_copy(q, d).wait_recv()
                total = total + from_late[d - 1].astype(F32)
            full[core, z_rows(q, z)] = total.astype(BF16)
            for d in range(1, nz):
                spread_copy(q, d).start()

        when_owner(q, z, action)

    def relay(q):
        for d in range(1, nz):
            when_owner(q, z_peer(nz - d), lambda d=d: spread_copy_from(q, d).wait_recv())
        if q != CROSSED:
            relay_copy(q, core).start()

    def small_step(step):
        if step == 0:
            small_core_copy.wait_recv()
            value = (small[core] + small_core[...]).astype(BF16)
            small_part[...] = value
            small_z[z] = value
            for d in range(1, nz):
                small_z_copy(d).start()
        elif step == 1:
            for d in range(1, nz):
                small_z_copy(d).wait_recv()
            total = small_z[0].astype(F32)
            for p in range(1, nz):
                total = total + small_z[p].astype(F32)
            value = total.astype(BF16)
            small_sum[...] = value
            small_seq[pos] = value
            for d in range(1, ns):
                small_seq_copy(d).start()
        else:
            for d in range(1, ns):
                small_seq_copy(d).wait_recv()
            total = small_seq[0].astype(F32)
            for p in range(1, ns):
                total = total + small_seq[p].astype(F32)
            small_all[core] = total
            small_done_copy(core).start()

    events = {"s": seq_done, "z": z_done, "f": early_done, "g": late_done, "a": relay, "m": small_step}
    for event in SEQUENCE:
        events[event[0]](int(event[1]))

    small_done_copy(core).wait_send()
    small_done_copy(1 - core).wait_recv()
    for h in range(2):
        grad_one_out[:, h * middle : (h + 1) * middle] = small_all[h, 0:TAPS]
        norms_out[:, h * middle : (h + 1) * middle] = small_all[h, 10:14]

    small_core_copy.wait_send()
    for d in range(1, nz):
        small_z_copy(d).wait_send()
    for d in range(1, ns):
        small_seq_copy(d).wait_send()
    halo_copy.wait_send()
    patch_copy.wait_send()
    for which in range(2):
        dpre_copy(which).wait_send()
    for q in range(len(parts)):
        if q in early:
            for d in range(1, nz):
                when_owner(q, z_peer(d), lambda q=q, d=d: early_copy(q, d).wait_send())
        else:
            for d in range(1, ns):
                seq_copy(q, d).wait_send()
            for d in range(1, nz):
                when_owner(q, z_peer(d), lambda q=q, d=d: z_copy(q, d).wait_send())

        def sent(q=q):
            if q in early:
                for d in range(1, ns):
                    late_copy(q, d).wait_send()
            for d in range(1, nz):
                spread_copy(q, d).wait_send()
            if q == CROSSED:
                for d in range(nz):
                    cross_copy(q, d).wait_send()

        when_owner(q, z, sent)
    for q in [int(event[1]) for event in SEQUENCE if event[0] == "a"]:
        start, size = parts[q]
        grad_two_out[start : start + size, pl.ds(pl.multiple_of(core * middle, 128), middle)] = full[core, part_rows(q)]
        if q == CROSSED:
            for d in range(nz):
                when_owner(q, z_peer(nz - d), lambda d=d: cross_copy_from(q, d).wait_recv())
        else:
            relay_copy(q, core).wait_send()
            relay_copy(q, 1 - core).wait_recv()
        grad_two_out[start : start + size, pl.ds(pl.multiple_of((1 - core) * middle, 128), middle)] = full[
            1 - core, part_rows(q)
        ]


def on_device(ns, nz, waveform, lengths, conv_one, conv_two, gain_one, shift_one, gain_two, shift_two, cotangent):
    clips, samples = waveform.shape
    channels = conv_two.shape[1]
    half = cotangent.shape[1]
    rows = clips * half
    block = conv_two.shape[0] // ns
    unit = block // 6
    parts = tuple(
        (sum(size for size, _ in PLAN[:q]) * unit, size * unit) for q, (size, _) in enumerate(PLAN)
    )
    early = tuple(q for q, (_, over_z) in enumerate(PLAN) if over_z)
    count = len(parts)
    piece = max(size // min(nz, size // 16) for _, size in parts)
    early_piece = max(parts[q][1] // min(nz, parts[q][1] // 16) for q in early)
    middle = channels // 2
    dma = pltpu.SemaphoreType.DMA
    vmem = pl.BlockSpec(memory_space=pltpu.VMEM)
    hbm = pl.BlockSpec(memory_space=pltpu.HBM)
    features, grad_one, grad_two, norms = pl.pallas_call(
        functools.partial(kernel, ns, nz, parts, early),
        out_shape=(
            jax.ShapeDtypeStruct((rows, channels), BF16),
            jax.ShapeDtypeStruct((TAPS, channels), F32),
            jax.ShapeDtypeStruct((block, channels), BF16),
            jax.ShapeDtypeStruct((4, channels), F32),
        ),
        in_specs=[hbm] * 9,
        out_specs=(vmem,) * 4,
        scratch_shapes=[
            pltpu.VMEM(waveform.shape, BF16),
            pltpu.SMEM(lengths.shape, jnp.int32),
            pltpu.VMEM(conv_one.shape, BF16),
            pltpu.VMEM(conv_two.shape, BF16),
            pltpu.VMEM((1, channels), F32),
            pltpu.VMEM((1, channels), F32),
            pltpu.VMEM((1, channels), F32),
            pltpu.VMEM((1, channels), F32),
            pltpu.VMEM((rows, channels), BF16),
            dma((9,)),
            pltpu.VMEM((clips, 128), BF16),
            pltpu.VMEM((2 * rows, 128), F32),
            pltpu.VMEM((2 * rows, channels), F32),
            pltpu.VMEM((2 * rows, channels), F32),
            pltpu.VMEM((2 * rows, 128), F32),
            pltpu.VMEM((2 * rows, channels), F32),
            pltpu.VMEM((rows + 8, channels), F32),
            pltpu.VMEM((2 * rows, 3 * channels), BF16),
            pltpu.VMEM((rows, channels), F32),
            pltpu.VMEM((2, rows, middle), BF16),
            pltpu.VMEM((rows, middle), BF16),
            pltpu.VMEM((rows + 8, channels), F32),
            pltpu.VMEM((2 * rows, channels), F32),
            pltpu.VMEM((2 * rows, channels), BF16),
            pltpu.VMEM((2 * rows, channels), BF16),
            pltpu.VMEM((rows, rows), BF16),
            pltpu.VMEM((rows, channels), F32),
            pltpu.VMEM((rows, channels), BF16),
            pltpu.VMEM((2, samples, 128), BF16),
            pltpu.VMEM((ns, max(parts[q][1] for q in early), middle), F32),
            pltpu.VMEM((ns, block, middle), BF16),
            pltpu.VMEM((ns - 1, block, middle), BF16),
            pltpu.VMEM((block, middle), BF16),
            pltpu.VMEM((count, nz - 1, piece, middle), BF16),
            pltpu.VMEM((nz - 1, ns, early_piece, middle), BF16),
            pltpu.VMEM((ns, early_piece, middle), BF16),
            pltpu.VMEM((ns - 1, early_piece, middle), BF16),
            pltpu.VMEM((2, block, middle), BF16),
            pltpu.VMEM((2, 16, middle), F32),
            pltpu.VMEM((16, middle), F32),
            pltpu.VMEM((16, middle), BF16),
            pltpu.VMEM((ns, 16, middle), BF16),
            pltpu.VMEM((16, middle), BF16),
            pltpu.VMEM((nz, 16, middle), BF16),
            pltpu.VMEM((2, 16, middle), F32),
            dma, dma,
            dma, dma,
            dma((2,)), dma((2,)),
            dma((count, ns - 1)), dma((count, ns - 1)),
            dma((count, nz - 1)), dma((count, nz - 1)),
            dma((count, nz - 1)), dma((count, nz - 1)),
            dma((count,)), dma((count,)),
            dma((nz,)), dma((nz,)),
            dma, dma,
            dma((ns - 1,)), dma((ns - 1,)),
            dma((nz - 1,)), dma((nz - 1,)),
            dma, dma,
        ],
        compiler_params=pltpu.CompilerParams(
            collective_id=0, has_side_effects=True, vmem_limit_bytes=48 * 1024 * 1024
        ),
    )(
        *[
            pltpu.with_memory_space_constraint(value, pltpu.HBM)
            for value in (
        waveform,
        lengths,
        conv_one,
        conv_two,
        gain_one.reshape(1, channels),
        shift_one.reshape(1, channels),
        gain_two.reshape(1, channels),
        shift_two.reshape(1, channels),
        cotangent.reshape(rows, channels),
    )])
    features, grad_one, grad_two, norms = pl.pallas_call(
        put_out,
        out_shape=(
            jax.ShapeDtypeStruct((rows, channels), BF16),
            jax.ShapeDtypeStruct((TAPS, channels), F32),
            jax.ShapeDtypeStruct((block, channels), F32),
            jax.ShapeDtypeStruct((4, channels), F32),
        ),
        in_specs=[vmem] * 4,
        out_specs=(hbm,) * 4,
        scratch_shapes=[pltpu.VMEM((block, channels), F32), dma((6,))],
        compiler_params=pltpu.CompilerParams(vmem_limit_bytes=4 * 1024 * 1024),
    )(features, grad_one, grad_two, norms)
    return features.reshape(clips, half, channels), grad_one, grad_two, norms


def put_out(features, grad_one, grad_two, norms, features_out, grad_one_out, grad_two_out, norms_out, wide, sem):
    rows = wide.shape[0] // 3
    copies = [
        pltpu.make_async_copy(source, target, sem.at[i])
        for i, (source, target) in enumerate(
            ((features, features_out), (grad_one, grad_one_out), (norms, norms_out))
        )
    ]
    for copy in copies:
        copy.start()
    for i in range(3):
        part = pl.ds(i * rows, rows)
        wide[part] = grad_two[part].astype(F32)
        copies.append(pltpu.make_async_copy(wide.at[part], grad_two_out.at[part], sem.at[3 + i]))
        copies[-1].start()
    for copy in copies:
        copy.wait()


def solution(mesh):
    in_specs = (P("dp", "seq"), P("dp", None), P(), P(), P(), P(), P(), P(), P("dp", "seq", None))
    out_specs = (P("dp", "seq", None), P(), P("seq", None), P())
    return jax.shard_map(
        functools.partial(on_device, mesh.shape["seq"], mesh.shape["dp"] // 2),
        mesh=mesh, in_specs=in_specs, out_specs=out_specs, check_vma=False,
    )
```
